128 devices in a mesh: gx: 16 (over z, y), gy: 8 (over x, core).
Axes of the slice: x: 4, y: 4, z: 4, core: 2. Of those that a mesh axis runs over, the one named last changes fastest.
Arguments:
- atmospheric_constituents: float32 [5, 72, 64, 2048], P(None, None, 'gy', 'gx'), may hold values from 0.001 to 2
- thermal_ratio: float32 [72, 64, 2048], P(None, 'gy', 'gx'), may hold values from 0.5 to 1.5
- flow_velocity: float32 [2, 72, 64, 2048], P(None, None, 'gy', 'gx'), may hold values from -4 to 4
- solar_elevation_factor: float32 [64, 2048], P('gy', 'gx'), may hold values from 0.1 to 1
- ground_reflectivity: float32 [64, 2048], P('gy', 'gx'), may hold values from 0.05 to 0.6
- sunlit_indicator: int32 [64, 2048], P('gy', 'gx'), may hold values from 0 to 1, as said below
- molecular_optics_lookup: float32 [3, 112, 72], replicated, may hold values from 0.0001 to 0.05
- condensate_optics_lookup: float32 [7, 112], replicated, may hold values from 0.1 to 0.9
Outputs:
- radiative_warming_rate: float32 [72, 64, 2048], P(None, 'gy', 'gx')
- advected_thermal_ratio: float32 [72, 64, 2048], P(None, 'gy', 'gx')
The draws below stay inside these ranges and needn't reach their ends.
Inputs may be any that keep to these rules, and one draw needn't show every extreme that they name: `sunlit_indicator`: A column's flag and that of the column 1024 further along the last dimension in the same row (round the end) sum to one.
All inputs are finite; a program needn't handle non-finite values.
Results may differ from the reference program's by a relative error of at most 0.0003.
Values sent between devices are 32-bit elements; how exact they have to be, the bound alone decides.
A program may use at most 128 MiB of HBM per device.

```python
import math
import jax
import jax.numpy as jnp
import numpy as np
from jax import lax

LEVEL_NUMBER = 72
GPOINTS = 112
NODES = 4
POINTS_EASTWARD = 2048
POINTS_NORTHWARD = 64


def draw_sunlit_indicator(key, part):
    shift_key = jax.random.fold_in(key, 11)
    pick_key = jax.random.fold_in(key, 12)
    shift_phase = jax.random.randint(shift_key, (), 0, 2000)
    chance = jax.random.randint(pick_key, (POINTS_NORTHWARD, POINTS_EASTWARD // 2), 0, 1000)
    positions = jnp.arange(POINTS_EASTWARD // 2, dtype=jnp.int32)
    phase = (positions * 2000 // POINTS_EASTWARD + shift_phase) % 2000
    triangle = jnp.abs(phase - 1000)
    threshold = jnp.clip(2 * triangle - 500, 0, 1000)
    first_half = (chance < threshold[None, :]).astype(jnp.int32)
    return jnp.concatenate([first_half, 1 - first_half], axis=1)


def log_between(key, shape, lowest, highest):
    unit = jax.random.uniform(key, shape, jnp.float32)
    return jnp.exp(jnp.log(lowest) + unit * (jnp.log(highest) - jnp.log(lowest)))


def draw_atmospheric_constituents(key, part):
    gas_key = jax.random.fold_in(key, 21)
    column_key = jax.random.fold_in(key, 22)
    layer_key = jax.random.fold_in(key, 23)
    cloud_key = jax.random.fold_in(key, 24)
    trace_key = jax.random.fold_in(key, 25)
    gas_shape = (3, LEVEL_NUMBER, POINTS_NORTHWARD, POINTS_EASTWARD)
    water_shape = (2, LEVEL_NUMBER, POINTS_NORTHWARD, POINTS_EASTWARD)
    column_pick = jax.random.uniform(column_key, (POINTS_NORTHWARD, POINTS_EASTWARD), jnp.float32)
    layer_pick = jax.random.uniform(layer_key, water_shape, jnp.float32)
    gas_part = log_between(gas_key, gas_shape, 0.1, 2.0)
    cloud_part = log_between(cloud_key, water_shape, 0.1, 2.0)
    trace_part = log_between(trace_key, water_shape, 0.001, 0.02)
    cloudy = (column_pick < 0.35)[None, None, :, :] & (layer_pick < 0.3)
    water_part = jnp.where(cloudy, cloud_part, trace_part)
    return jnp.concatenate([gas_part, water_part], axis=0).astype(jnp.float32)


def levels(rng, shape, cuts, smallest, top_value):
    level, own = 1.0, jax.random.fold_in(rng, 6)
    for dim, parts in cuts:
        draws = jnp.exp(jax.random.uniform(jax.random.fold_in(own, dim), (parts,), jnp.float32, smallest / len(cuts), top_value / len(cuts)))
        level = level * jnp.repeat(draws, shape[dim] // parts).reshape([-1 if axis == dim else 1 for axis in range(len(shape))])
    return level


def normal_values(stream_key, extent, width, most, shards=(), kind=jnp.bfloat16):
    result = jax.random.normal(stream_key, extent, jnp.float32) * width
    if len(shards) > 0:
        result = levels(stream_key, extent, shards, -0.22, 0.18) * result
    return jnp.clip(result, min=-most, max=most).astype(kind)


def setup_inputs(seed: int = 0) -> dict:
    keys = jax.random.split(jax.random.key(seed), 9)
    return {
        "atmospheric_constituents": draw_atmospheric_constituents(jax.random.fold_in(keys[8], 71), 0),
        "thermal_ratio": jnp.clip(0.5 + 1.0 * jax.random.uniform(keys[1], (LEVEL_NUMBER, POINTS_NORTHWARD, POINTS_EASTWARD), jnp.float32) ** levels(keys[1], (LEVEL_NUMBER, POINTS_NORTHWARD, POINTS_EASTWARD), ((1, 8), (2, 16)), -0.2, 0.2), 0.5, 1.5),
        "flow_velocity": normal_values(keys[2], (2, LEVEL_NUMBER, POINTS_NORTHWARD, POINTS_EASTWARD), 1.0, 4.0, ((2, 8), (3, 16)), jnp.float32),
        "solar_elevation_factor": jnp.clip(0.1 + 0.9 * jax.random.uniform(keys[3], (POINTS_NORTHWARD, POINTS_EASTWARD), jnp.float32) ** levels(keys[3], (POINTS_NORTHWARD, POINTS_EASTWARD), ((0, 8), (1, 16)), -0.2, 0.2), 0.1, 1.0),
        "ground_reflectivity": jnp.clip(0.05 + 0.55 * jax.random.uniform(keys[4], (POINTS_NORTHWARD, POINTS_EASTWARD), jnp.float32) ** levels(keys[4], (POINTS_NORTHWARD, POINTS_EASTWARD), ((0, 8), (1, 16)), -0.2, 0.2), 0.05, 0.6),
        "sunlit_indicator": draw_sunlit_indicator(jax.random.fold_in(keys[8], 71), 0),
        "molecular_optics_lookup": jnp.clip(jnp.exp(jax.random.uniform(keys[6], (3, GPOINTS, LEVEL_NUMBER), jnp.float32, math.log(0.0001), math.log(0.05))), 0.0001, 0.05),
        "condensate_optics_lookup": jnp.clip(jax.random.uniform(keys[7], (7, GPOINTS), jnp.float32, 0.1, 0.9), 0.1, 0.9),
    }


TIME_INCREMENT = 0.05

def gll_derivative():
    points = np.array([-1.0, -1.0 / np.sqrt(5.0), 1.0 / np.sqrt(5.0), 1.0])
    legendre = 0.5 * (5.0 * points ** 3 - 3.0 * points)
    derivative = np.zeros((4, 4))
    for source in range(4):
        for target in range(4):
            if source != target:
                derivative[source, target] = legendre[source] / (legendre[target] * (points[source] - points[target]))
    derivative[0, 0] = -3.0
    derivative[3, 3] = 3.0
    return derivative

def depth_terms(coeffs, optics_table, columns):
    vapour, ozone_amount, thickness, liquid, frozen, temper = columns
    weighted = thickness * temper * temper
    gas_depth = coeffs[0][:, None] * (weighted * vapour)[None, :] + coeffs[1][:, None] * (weighted * ozone_amount)[None, :]
    rayleigh = coeffs[2][:, None] * thickness[None, :]
    liquid_depth = optics_table[0][:, None] * liquid[None, :]
    ice_depth = optics_table[3][:, None] * frozen[None, :]
    liquid_scatter = optics_table[1][:, None] * liquid_depth
    ice_scatter = optics_table[4][:, None] * ice_depth
    scattering = rayleigh + liquid_scatter + ice_scatter
    absorption = gas_depth + (liquid_depth - liquid_scatter) + (ice_depth - ice_scatter)
    forward = optics_table[2][:, None] * liquid_scatter + optics_table[5][:, None] * ice_scatter
    return (scattering, absorption, forward)

def layer_optics(coeffs, optics_table, columns, cosine):
    scattering, absorption, forward = depth_terms(coeffs, optics_table, columns)
    optical_depth = scattering + absorption
    single_albedo = scattering / optical_depth
    asymmetry = forward / scattering
    eigen_rate = 2.0 * jnp.sqrt(absorption / optical_depth * (1.0 - single_albedo * asymmetry))
    gamma_one = 2.0 - single_albedo * (1.0 + asymmetry)
    gamma_two = single_albedo * (1.0 - asymmetry)
    shrink = jnp.expm1(-eigen_rate * optical_depth)
    decay_factor = 1.0 + shrink
    spread = -shrink * (2.0 + shrink)
    denominator = gamma_one * spread + eigen_rate * (1.0 + decay_factor * decay_factor)
    reflect = gamma_two * spread / denominator
    transmit = 2.0 * eigen_rate * decay_factor / denominator
    beam_loss = jnp.expm1(-optical_depth / cosine[None, :])
    direct = 1.0 + beam_loss
    reflect_beam = -0.5 * single_albedo * beam_loss * (1.0 - asymmetry)
    transmit_beam = -0.5 * single_albedo * beam_loss * (1.0 + asymmetry)
    return (reflect, transmit, reflect_beam, transmit_beam, direct)

def pair_average(values, axis_index):
    count = values.shape[axis_index]
    before = jnp.roll(values, 1, axis_index)
    beyond = jnp.roll(values, -1, axis_index)
    node_index = jnp.arange(count) % NODES
    if axis_index == 2:
        node_index = node_index[None, None, :]
    else:
        node_index = node_index[None, :, None]
    return jnp.where(node_index == NODES - 1, 0.5 * (values + beyond), jnp.where(node_index == 0, 0.5 * (before + values), values))

def reference(atmospheric_constituents, thermal_ratio, flow_velocity, solar_elevation_factor, ground_reflectivity, sunlit_indicator, molecular_optics_lookup, condensate_optics_lookup):
    level_coeffs = jnp.moveaxis(molecular_optics_lookup, 2, 0)

    def warming_rate_each_line(inputs):
        state_row, temp_row, cosine, ground, day_flags = inputs

        def level_optics(per_level):
            return layer_optics(per_level[0], condensate_optics_lookup, per_level[1:], cosine)
        reflect, transmit, reflect_beam, transmit_beam, direct = lax.map(level_optics, (level_coeffs, state_row[0], state_row[1], state_row[2], state_row[3], state_row[4], temp_row))
        plane = reflect.shape[1:]

        def beam_step(beam_flux, direct_now):
            return (beam_flux * direct_now, beam_flux)
        surface_beam, beams = lax.scan(beam_step, jnp.broadcast_to(cosine[None, :], plane), direct)
        ground_full = jnp.broadcast_to(ground[None, :], plane)

        def below_step(below, per_level):
            albedo_below, source_below = below
            reflect_now, transmit_now, rbeam_now, tbeam_now, beam_now = per_level
            inverse = 1.0 / (1.0 - reflect_now * albedo_below)
            albedo_here = reflect_now + transmit_now * transmit_now * albedo_below * inverse
            source_here = beam_now * rbeam_now + transmit_now * inverse * (source_below + albedo_below * beam_now * tbeam_now)
            return ((albedo_here, source_here), (albedo_here, source_here, albedo_below, source_below))
        _, (albedos, sources, albedo_next, source_next) = lax.scan(below_step, (ground_full, ground_full * surface_beam), (reflect, transmit, reflect_beam, transmit_beam, beams), reverse=True)

        def down_step(diffuse_now, per_level):
            reflect_now, transmit_now, tbeam_now, beam_now, albedo_after, source_after = per_level
            diffuse_new = (transmit_now * diffuse_now + beam_now * tbeam_now + reflect_now * source_after) / (1.0 - reflect_now * albedo_after)
            return (diffuse_new, diffuse_new)
        _, diffuse = lax.scan(down_step, jnp.zeros_like(ground_full), (reflect, transmit, transmit_beam, beams, albedo_next, source_next))
        beam_all = jnp.concatenate([beams, surface_beam[None]], axis=0)
        albedo_all = jnp.concatenate([albedos, ground_full[None]], axis=0)
        source_all = jnp.concatenate([sources, (ground_full * surface_beam)[None]], axis=0)
        diffuse_all = jnp.concatenate([jnp.zeros_like(ground_full)[None], diffuse], axis=0)
        net_flux = beam_all + diffuse_all - (albedo_all * diffuse_all + source_all)
        interface = lax.optimization_barrier(jnp.sum(condensate_optics_lookup[6][None, :, None] * net_flux, axis=1))
        heating_row = LEVEL_NUMBER / GPOINTS * (interface[:-1] - interface[1:])
        return jnp.where(day_flags[None, :] == 1, heating_row, 0.0)
    warming_rate_lines = lax.map(warming_rate_each_line, (jnp.moveaxis(atmospheric_constituents, 2, 0), jnp.moveaxis(thermal_ratio, 1, 0), solar_elevation_factor, ground_reflectivity, sunlit_indicator))
    radiative_warming_rate = jnp.moveaxis(warming_rate_lines, 0, 1)
    derivative = jnp.asarray(gll_derivative(), jnp.float32)

    def warming_change_rate(field_now):
        level_sum_entries, rows_all, width_all = field_now.shape
        blocks_x = field_now.reshape(level_sum_entries, rows_all, width_all // NODES, NODES)
        slope_x = jnp.einsum('ij,lyej->lyei', derivative, blocks_x, precision=lax.Precision.HIGHEST).reshape(field_now.shape)
        blocks_y = field_now.reshape(level_sum_entries, rows_all // NODES, NODES, width_all)
        slope_y = jnp.einsum('ij,lejx->leix', derivative, blocks_y, precision=lax.Precision.HIGHEST).reshape(field_now.shape)
        raw = radiative_warming_rate - (flow_velocity[0] * slope_x + flow_velocity[1] * slope_y)
        return pair_average(pair_average(raw, 2), 1)
    opening_advection_part = thermal_ratio + TIME_INCREMENT * warming_change_rate(thermal_ratio)
    middle_advection_part = 0.75 * thermal_ratio + 0.25 * (opening_advection_part + TIME_INCREMENT * warming_change_rate(opening_advection_part))
    advected_thermal_ratio = 1.0 / 3.0 * thermal_ratio + 2.0 / 3.0 * (middle_advection_part + TIME_INCREMENT * warming_change_rate(middle_advection_part))
    return (radiative_warming_rate, advected_thermal_ratio)
```

```python
import functools

import jax
import jax.numpy as jnp
import numpy as np
from jax import lax
from jax.experimental import pallas as pl
from jax.experimental.pallas import tpu as pltpu
from jax.sharding import PartitionSpec as P

NODES = 4


TIME_INCREMENT = 0.05


def shifted(value, axis, steps):
    count = lax.axis_size(axis)
    pairs = [(source, (source + steps) % count) for source in range(count)]
    return lax.ppermute(value, axis, pairs)


def padded_2(block, sides, width):
    for axis, dim in sides:
        count = lax.axis_size(axis)
        forward = [(i, i + 1) for i in range(count - 1)]
        forward.append((count - 1, 0))
        backward = [(target, source) for source, target in forward]
        low = lax.ppermute(
            lax.slice_in_dim(block, block.shape[dim] - width, None, axis=dim), axis, forward
        )
        high = lax.ppermute(lax.slice_in_dim(block, 0, width, axis=dim), axis, backward)
        block = jnp.concatenate([low, block, high], axis=dim)
    return block


def gll_derivative():
    points = np.array([-1.0, -1.0 / np.sqrt(5.0), 1.0 / np.sqrt(5.0), 1.0])
    legendre = 0.5 * (5.0 * points**3 - 3.0 * points)
    derivative = np.zeros((4, 4))
    for source in range(4):
        for target in range(4):
            if source != target:
                derivative[source, target] = legendre[source] / (
                    legendre[target] * (points[source] - points[target])
                )
    derivative[0, 0] = -3.0
    derivative[3, 3] = 3.0
    return derivative


LOG2E = 1.4426950408889634


def coef_matrix(mol, tab):
    g, levels = mol.shape[1], mol.shape[2]
    k0, k1, k2 = mol[0].T, mol[1].T, mol[2].T
    zero = jnp.zeros_like(k0)
    full = lambda v: jnp.broadcast_to(v[None, :], k0.shape)
    lext, lalb, lasy, iext, ialb, iasy = (tab[i] for i in range(6))
    depth = jnp.stack([k0, k1, k2, full(lext), full(iext), zero, zero, zero], -1) * 2.0
    absorb = jnp.stack([k0, k1, zero, full(lext * (1 - lalb)), full(iext * (1 - ialb)), zero, zero, zero], -1)
    back = jnp.stack([zero, zero, k2, full(lext * lalb * (1 - lasy)), full(iext * ialb * (1 - iasy)), zero, zero, zero], -1)
    c = jnp.concatenate([depth, absorb, back], axis=1)
    hi = lax.reduce_precision(c, 8, 7)
    lo = c - hi
    z = jnp.zeros_like(hi)
    return jnp.concatenate([hi, hi, lo, z], axis=-1).astype(jnp.bfloat16)


def recip(x, exact):
    return pl.reciprocal(x, approx=not exact)


def rad_kernel(exact, x_ref, sfc_ref, lhs_ref, w_ref, out_ref, mm, beam, src, a_all, p_all, o_all, flux):
    levels, gtot, n = p_all.shape
    blocks = gtot // 8
    mu = sfc_ref[0:1, :]
    ground = sfc_ref[1:2, :]
    nc = jnp.broadcast_to((-0.5 * LOG2E) / mu, (8, n))

    def mults(l, slot):
        x = x_ref[l]
        hi = x.astype(jnp.bfloat16).astype(jnp.float32)
        lo = x - hi
        rhs = jnp.concatenate([hi, lo, hi, jnp.zeros_like(hi)], axis=0).astype(jnp.bfloat16)
        mm[slot] = jnp.dot(lhs_ref[l], rhs, preferred_element_type=jnp.float32)

    mults(0, 0)
    acc = jnp.zeros((8, n), jnp.float32)
    for i in range(blocks):
        sl = pl.ds(8 * i, 8)
        b0 = w_ref[sl, :n] * mu
        beam[sl, :] = b0
        src[sl, :] = jnp.zeros((8, n), jnp.float32)
        a_all[0, sl, :] = jnp.zeros((8, n), jnp.float32)
        acc = acc + b0
    flux[0:1, :] = jnp.sum(acc, axis=0, keepdims=True)

    def down(l, slot):
        acc = jnp.zeros((8, n), jnp.float32)
        for i in range(blocks):
            sl = pl.ds(8 * i, 8)
            t2 = mm[slot, sl, :]
            a = mm[slot, pl.ds(gtot + 8 * i, 8), :]
            b = mm[slot, pl.ds(2 * gtot + 8 * i, 8), :]
            bm = beam[sl, :]
            s = src[sl, :]
            alb = a_all[l, sl, :]
            c = a + b
            pr = a * c
            q = pr * lax.rsqrt(pr)
            t = jnp.tanh(q)
            u = q * (t * t)
            x = a + c
            rden = recip(t * x + (q + u), exact)
            refl = (t * b) * rden
            tran = (q - u) * rden
            bn = bm * jnp.exp2(t2 * nc)
            lost = bm - bn
            w = lost * recip(t2, exact)
            rb = w * b
            tb = lost - w * x
            inv = recip(1.0 - refl * alb, exact)
            p = tran * inv
            o = (refl * s + rb) * inv
            a1 = refl + (tran * alb) * p
            s1 = tb + p * (s + alb * rb)
            p_all[l, sl, :] = p
            o_all[l, sl, :] = o
            a_all[l + 1, sl, :] = a1
            beam[sl, :] = bn
            src[sl, :] = s1
            acc = acc + (bn + s1)
        flux[pl.ds(l + 1, 1), :] = jnp.sum(acc, axis=0, keepdims=True)

    @pl.loop(0, levels // 2)
    def _(h):
        l = 2 * h
        mults(l + 1, 1)
        down(l, 0)
        mults(jnp.minimum(l + 2, levels - 1), 0)
        down(l + 1, 1)

    us = []
    acc = jnp.zeros((8, n), jnp.float32)
    for i in range(blocks):
        sl = pl.ds(8 * i, 8)
        alb = a_all[levels, sl, :]
        up = ground * (src[sl, :] + beam[sl, :]) * (1.0 / (1.0 - ground * alb))
        us.append(up)
        acc = acc + (1.0 - alb) * up
    flux[levels:levels + 1, :] = flux[levels:levels + 1, :] - jnp.sum(acc, axis=0, keepdims=True)

    def upward(k, us):
        l = levels - 1 - k
        acc = jnp.zeros((8, n), jnp.float32)
        out = []
        for i in range(blocks):
            sl = pl.ds(8 * i, 8)
            up = p_all[l, sl, :] * us[i] + o_all[l, sl, :]
            acc = acc + (1.0 - a_all[l, sl, :]) * up
            out.append(up)
        flux[pl.ds(l, 1), :] = flux[pl.ds(l, 1), :] - jnp.sum(acc, axis=0, keepdims=True)
        return tuple(out)

    lax.fori_loop(0, levels, upward, tuple(us))
    out_ref[...] = (levels / gtot) * (flux[0:levels, :] - flux[1:levels + 1, :])


def rad(x, sfc, lhs, wb, exact=True):
    levels, _, n = x.shape
    gtot = wb.shape[0]
    f32 = jnp.float32
    return pl.pallas_call(
        functools.partial(rad_kernel, exact),
        out_shape=jax.ShapeDtypeStruct((levels, n), f32),
        in_specs=[pl.BlockSpec(memory_space=pltpu.VMEM)] * 4,
        out_specs=pl.BlockSpec(memory_space=pltpu.VMEM),
        scratch_shapes=[
            pltpu.VMEM((2, 3 * gtot, n), f32),
            pltpu.VMEM((gtot, n), f32),
            pltpu.VMEM((gtot, n), f32),
            pltpu.VMEM((levels + 1, gtot, n), f32),
            pltpu.VMEM((levels, gtot, n), f32),
            pltpu.VMEM((levels, gtot, n), f32),
            pltpu.VMEM((levels + 8, n), f32),
        ],
        compiler_params=pltpu.CompilerParams(vmem_limit_bytes=56 * 2**20),
        name="shortwave",
    )(x, sfc, lhs, wb)


def pair_average(values, before, beyond, node_index):
    return jnp.where(
        node_index == NODES - 1,
        0.5 * (values + beyond),
        jnp.where(node_index == 0, 0.5 * (before + values), values),
    )


def local(
    atmospheric_constituents,
    thermal_ratio,
    flow_velocity,
    solar_elevation_factor,
    ground_reflectivity,
    sunlit_indicator,
    molecular_optics_lookup,
    condensate_optics_lookup,
):
    levels, lines, span = thermal_ratio.shape
    half = lines // 2
    partner = lax.axis_size("gx") // 2
    low = lax.axis_index("gx") < partner
    weighted = atmospheric_constituents[2] * thermal_ratio * thermal_ratio
    state = jnp.concatenate(
        [
            (weighted * atmospheric_constituents[0])[None],
            (weighted * atmospheric_constituents[1])[None],
            atmospheric_constituents[2:],
        ],
        axis=0,
    )
    surface = jnp.stack([solar_elevation_factor, ground_reflectivity])

    def mine(value):
        return jnp.where(low, value[..., :half, :], value[..., half:, :])

    def theirs(value):
        return jnp.where(low, value[..., half:, :], value[..., :half, :])

    got_state, got_surface = shifted((theirs(state), theirs(surface)), "gx", partner)
    day_here = mine(sunlit_indicator) == 1
    work_state = jnp.where(day_here, mine(state), got_state)
    work_surface = jnp.where(day_here, mine(surface), got_surface)
    pairs = half // 2
    columns = jnp.pad(work_state, ((0, 3), (0, 0), (0, 0), (0, 0)))
    columns = columns.reshape(8, levels, 2, pairs * span).transpose(2, 1, 0, 3)
    sfc = jnp.pad(work_surface, ((0, 6), (0, 0), (0, 0))).reshape(8, 2, pairs * span).transpose(1, 0, 2)
    lhs = coef_matrix(molecular_optics_lookup, condensate_optics_lookup)
    wide = jnp.broadcast_to(
        condensate_optics_lookup[6][:, None], (condensate_optics_lookup.shape[1], pairs * span)
    )
    heats = [rad(columns[h], sfc[h], lhs, wide).reshape(levels, pairs, span) for h in range(2)]
    work_heat = jnp.concatenate(heats, axis=1)
    returned = shifted(work_heat, "gx", partner)
    both = jnp.concatenate(
        [jnp.where(low, work_heat, returned), jnp.where(low, returned, work_heat)], axis=1
    )
    radiative_warming_rate = jnp.where(sunlit_indicator == 1, both, 0.0)
    resident_span_size = span
    resident_line_number = lines
    derivative = gll_derivative()
    x_derivative = jnp.asarray(
        np.kron(np.eye(resident_span_size // NODES), derivative).T, jnp.float32
    )
    y_derivative = jnp.asarray(
        np.kron(np.eye(resident_line_number // NODES), derivative), jnp.float32
    )
    x_nodes = (jnp.arange(resident_span_size) % NODES)[None, None, :]
    y_nodes = (jnp.arange(resident_line_number) % NODES)[None, :, None]

    def averaged(values):
        padded = padded_2(values, (("gx", 2),), 1)
        along_x = pair_average(values, padded[:, :, :-2], padded[:, :, 2:], x_nodes)
        padded_y = padded_2(along_x, (("gy", 1),), 1)
        return pair_average(along_x, padded_y[:, :-2], padded_y[:, 2:], y_nodes)

    def warming_change_rate(field_now):
        slope_x = jnp.dot(
            field_now.reshape(-1, resident_span_size), x_derivative, precision=lax.Precision.HIGHEST
        ).reshape(field_now.shape)
        slope_y = jnp.einsum(
            "ij,ljx->lix", y_derivative, field_now, precision=lax.Precision.HIGHEST
        )
        return averaged(
            radiative_warming_rate - (flow_velocity[0] * slope_x + flow_velocity[1] * slope_y)
        )

    opening_advection_part = thermal_ratio + TIME_INCREMENT * warming_change_rate(thermal_ratio)
    middle_advection_part = 0.75 * thermal_ratio + 0.25 * (
        opening_advection_part + TIME_INCREMENT * warming_change_rate(opening_advection_part)
    )
    advected_thermal_ratio = 1.0 / 3.0 * thermal_ratio + 2.0 / 3.0 * (
        middle_advection_part + TIME_INCREMENT * warming_change_rate(middle_advection_part)
    )
    return (radiative_warming_rate, advected_thermal_ratio)


def solution(mesh):
    in_specs = (
        P(None, None, "gy", "gx"),
        P(None, "gy", "gx"),
        P(None, None, "gy", "gx"),
        P("gy", "gx"),
        P("gy", "gx"),
        P("gy", "gx"),
        P(),
        P(),
    )
    out_specs = (P(None, "gy", "gx"), P(None, "gy", "gx"))
    return jax.shard_map(local, mesh=mesh, in_specs=in_specs, out_specs=out_specs, check_vma=False)
```

```python
import functools

import jax
import jax.numpy as jnp
import numpy as np
from jax import lax
from jax.experimental import pallas as pl
from jax.experimental.pallas import tpu as pltpu
from jax.sharding import PartitionSpec as P

NODES = 4
TIME_INCREMENT = 0.05
LOG2E = 1.4426950408889634
MESH = pl.DeviceIdType.MESH
FIELDS = 5
PACK = 4


def gll_derivative():
    points = np.array([-1.0, -1.0 / np.sqrt(5.0), 1.0 / np.sqrt(5.0), 1.0])
    legendre = 0.5 * (5.0 * points**3 - 3.0 * points)
    derivative = np.zeros((4, 4))
    for source in range(4):
        for target in range(4):
            if source != target:
                derivative[source, target] = legendre[source] / (
                    legendre[target] * (points[source] - points[target])
                )
    derivative[0, 0] = -3.0
    derivative[3, 3] = 3.0
    return derivative


def coef_matrix(mol, tab):
    k0, k1, k2 = mol[0].T, mol[1].T, mol[2].T
    levels, gpoints = k0.shape
    zero = jnp.zeros_like(k0)
    lext, lalb, lasy, iext, ialb, iasy = (
        jnp.broadcast_to(tab[i][None, :], k0.shape) for i in range(6)
    )
    pad = [zero] * 3
    depth = jnp.stack([2 * k0, 2 * k1, 2 * k2, 2 * lext, 2 * iext] + pad, -1)
    absorb = jnp.stack([k0, k1, zero, lext * (1 - lalb), iext * (1 - ialb)] + pad, -1)
    back = jnp.stack(
        [zero, zero, k2, lext * lalb * (1 - lasy), iext * ialb * (1 - iasy)] + pad, -1
    )
    coefs = jnp.concatenate([depth, absorb, back], axis=1)
    high = lax.reduce_precision(coefs, 8, 7)
    low = coefs - high
    wide = jnp.concatenate([high, high, low, jnp.zeros_like(high)], axis=-1)
    wide = wide.reshape(levels // PACK, PACK, 3 * gpoints, 32).transpose(0, 2, 1, 3)
    return wide.reshape(levels // PACK, 3 * gpoints, PACK * 32).astype(jnp.bfloat16)


def shortwave(x_ref, mu, ground, lhs_ref, w_ref, out_ref, mm, beam, src, a_all, p_all, o_all, flux):
    levels, gtot, n = p_all.shape
    blocks = gtot // 8
    f32 = jnp.float32
    nc = jnp.broadcast_to((-0.5 * LOG2E) / mu, (8, n))

    def mults(l, slot):
        x = jnp.concatenate(
            [x_ref[r, pl.ds(l, 8, stride=levels), :] for r in range(x_ref.shape[0])], axis=1
        )
        high = x.astype(jnp.bfloat16).astype(f32)
        low = x - high
        nil = jnp.zeros_like(high)
        inner = lax.rem(l, PACK)
        parts = []
        for j in range(PACK):
            hit = inner == j
            h = jnp.where(hit, high, nil)
            parts += [h, jnp.where(hit, low, nil), h, nil]
        rhs = jnp.concatenate(parts, axis=0).astype(jnp.bfloat16)
        mm[slot] = jnp.dot(lhs_ref[l // PACK], rhs, preferred_element_type=f32)

    mults(0, 0)
    acc = jnp.zeros((8, n), f32)
    for i in range(blocks):
        sl = pl.ds(8 * i, 8)
        first = w_ref[sl, :] * mu
        beam[sl, :] = first
        src[sl, :] = jnp.zeros((8, n), f32)
        a_all[0, sl, :] = jnp.zeros((8, n), f32)
        acc = acc + first
    flux[0:1, :] = jnp.sum(acc, axis=0, keepdims=True)

    def down(l, slot):
        acc = jnp.zeros((8, n), f32)
        for i in range(blocks):
            sl = pl.ds(8 * i, 8)
            t2 = mm[slot, sl, :]
            a = mm[slot, pl.ds(gtot + 8 * i, 8), :]
            b = mm[slot, pl.ds(2 * gtot + 8 * i, 8), :]
            bm = beam[sl, :]
            s = src[sl, :]
            alb = a_all[l, sl, :]
            c = a + b
            pr = a * c
            q = pr * lax.rsqrt(pr)
            t = jnp.tanh(q)
            u = q * (t * t)
            x = a + c
            rden = 1.0 / (t * x + (q + u))
            refl = (t * b) * rden
            tran = (q - u) * rden
            bn = bm * jnp.exp2(t2 * nc)
            lost = bm - bn
            w = lost * (1.0 / t2)
            rb = w * b
            tb = lost - w * x
            inv = 1.0 / (1.0 - refl * alb)
            p = tran * inv
            o = (refl * s + rb) * inv
            a1 = refl + (tran * alb) * p
            s1 = tb + p * (s + alb * rb)
            p_all[l, sl, :] = p
            o_all[l, sl, :] = o
            a_all[l + 1, sl, :] = a1
            beam[sl, :] = bn
            src[sl, :] = s1
            acc = acc + (bn + s1)
        flux[pl.ds(l + 1, 1), :] = jnp.sum(acc, axis=0, keepdims=True)

    @pl.loop(0, levels // 2)
    def _(h):
        l = 2 * h
        mults(l + 1, 1)
        down(l, 0)
        mults(jnp.minimum(l + 2, levels - 1), 0)
        down(l + 1, 1)

    ups = []
    acc = jnp.zeros((8, n), f32)
    for i in range(blocks):
        sl = pl.ds(8 * i, 8)
        alb = a_all[levels, sl, :]
        up = ground * (src[sl, :] + beam[sl, :]) * (1.0 / (1.0 - ground * alb))
        ups.append(up)
        acc = acc + (1.0 - alb) * up
    last = pl.ds(levels, 1)
    flux[last, :] = flux[last, :] - jnp.sum(acc, axis=0, keepdims=True)

    def upward(k, ups):
        l = levels - 1 - k
        acc = jnp.zeros((8, n), f32)
        out = []
        for i in range(blocks):
            sl = pl.ds(8 * i, 8)
            up = p_all[l, sl, :] * ups[i] + o_all[l, sl, :]
            acc = acc + (1.0 - a_all[l, sl, :]) * up
            out.append(up)
        row = pl.ds(l, 1)
        flux[row, :] = flux[row, :] - jnp.sum(acc, axis=0, keepdims=True)
        return tuple(out)

    lax.fori_loop(0, levels, upward, tuple(ups))
    out_ref[...] = (levels / gtot) * (flux[0:levels, :] - flux[1 : levels + 1, :])


def whole_kernel(
    nx, ny, state_ref, temp_ref, flow_ref, mu_ref, ground_ref, day_ref, lhs_ref, w_ref,
    heat_ref, adv_ref,
    snd, got, xs, mm, beam, src, a_all, p_all, o_all, flux, hwork, hgot,
    raw, cur, rowsnd, rowgot, edgesnd, edgegot,
    state_send, state_recv, heat_send, heat_recv, halo_send, halo_recv,
):
    f32 = jnp.float32
    gx, gy = lax.axis_index("gx"), lax.axis_index("gy")
    lines, span = mu_ref.shape
    total = temp_ref.shape[0]
    levels = total // lines
    half = lines // 2
    pair = half // 2
    east, west = lax.rem(gx + 1, nx), lax.rem(gx + nx - 1, nx)
    south, north = lax.rem(gy + 1, ny), lax.rem(gy + ny - 1, ny)
    far = lax.rem(gx + nx // 2, nx)
    mine = jnp.where(gx < nx // 2, 0, half)
    theirs = half - mine

    targets = [
        (east, gy), (east, south), (east, north),
        (west, gy), (west, south), (west, north),
        (gx, south), (gx, north),
    ]
    barrier = pltpu.get_barrier_semaphore()
    for device in targets + [(far, gy)]:
        pl.semaphore_signal(barrier, inc=1, device_id=device, device_id_type=MESH)
    pl.semaphore_wait(barrier, len(targets) + 1)

    def products(line, store):
        line_of = lambda ref, k: ref[pl.ds(k * total + line, levels, stride=lines), :]
        temper = line_of(temp_ref, 0)
        thick = line_of(state_ref, 2)
        weighted = thick * temper * temper
        values = [
            weighted * line_of(state_ref, 0),
            weighted * line_of(state_ref, 1),
            thick,
            line_of(state_ref, 3),
            line_of(state_ref, 4),
        ]
        for k, value in enumerate(values):
            store(slice(k * levels, (k + 1) * levels), value)

    def state_copy(h):
        return pltpu.make_async_remote_copy(
            src_ref=snd.at[h], dst_ref=got.at[h], send_sem=state_send.at[h],
            recv_sem=state_recv.at[h], device_id=(far, gy), device_id_type=MESH,
        )

    def heat_copy(h):
        return pltpu.make_async_remote_copy(
            src_ref=hwork.at[h], dst_ref=hgot.at[h], send_sem=heat_send.at[h],
            recv_sem=heat_recv.at[h], device_id=(far, gy), device_id_type=MESH,
        )

    tail = FIELDS * levels
    for h in range(2):
        for r in range(pair):
            lanes = slice(r * span, (r + 1) * span)
            line = theirs + pair * h + r

            def to_send(rows, value, h=h, lanes=lanes):
                snd[h, rows, lanes] = value

            products(line, to_send)
            snd[h, tail : tail + 1, lanes] = mu_ref[pl.ds(line, 1), :]
            snd[h, tail + 1 : tail + 2, lanes] = ground_ref[pl.ds(line, 1), :]
            snd[h, tail + 2 : tail + 8, lanes] = jnp.zeros((6, span), f32)
        state_copy(h).start()

    for h in range(2):
        for r in range(pair):
            xs[h, r, tail:, :] = jnp.zeros((xs.shape[2] - tail, span), f32)

            def to_own(rows, value, h=h, r=r):
                xs[h, r, rows, :] = value

            products(mine + pair * h + r, to_own)

    dref = gll_derivative()
    lane = lax.broadcasted_iota(jnp.int32, (lines, span), 1)
    line_no = lax.broadcasted_iota(jnp.int32, (lines, span), 0)
    node_x, node_y = lane % NODES, line_no % NODES

    def taps(node):
        out = []
        for k in range(1 - NODES, NODES):
            coef = jnp.zeros((lines, span), f32)
            for i in range(NODES):
                if 0 <= i + k < NODES and dref[i, i + k] != 0.0:
                    coef = jnp.where(node == i, float(dref[i, i + k]), coef)
            out.append((k, coef))
        return out

    taps_x, taps_y = taps(node_x), taps(node_y)

    def slope(v, axis, size, table):
        out = None
        for k, coef in table:
            moved = v if k == 0 else pltpu.roll(v, (-k) % size, axis)
            out = coef * moved if out is None else out + coef * moved
        return out

    def at(l):
        return pl.ds(pl.multiple_of(l * lines, lines), lines)

    def wind(v, l):
        return flow_ref[at(l), :] * slope(v, 1, span, taps_x) + flow_ref[
            at(levels + l), :
        ] * slope(v, 0, lines, taps_y)

    group = 8

    @pl.loop(0, levels // group)
    def _(j):
        for i in range(group):
            l = j * group + i
            raw[at(l), :] = wind(temp_ref[at(l), :], l)

    for h in range(2):
        state_copy(h).wait_recv()
        mus, grounds = [], []
        for r in range(pair):
            lanes = slice(r * span, (r + 1) * span)
            line = pl.ds(mine + pair * h + r, 1)
            own = day_ref[line, :] == 1
            for k in range(FIELDS):
                rows = slice(k * levels, (k + 1) * levels)
                xs[h, r, rows, :] = jnp.where(own, xs[h, r, rows, :], got[h, rows, lanes])
            mus.append(jnp.where(own, mu_ref[line, :], got[h, tail : tail + 1, lanes]))
            grounds.append(jnp.where(own, ground_ref[line, :], got[h, tail + 1 : tail + 2, lanes]))
        shortwave(
            xs.at[h], jnp.concatenate(mus, axis=1), jnp.concatenate(grounds, axis=1),
            lhs_ref, w_ref, hwork.at[h], mm, beam, src, a_all, p_all, o_all, flux,
        )
        heat_copy(h).start()

    def place(source, first, h):
        for r in range(pair):
            line = first + pair * h + r
            own = day_ref[pl.ds(line, 1), :] == 1
            heat_ref[pl.ds(line, levels, stride=lines), :] = jnp.where(
                own, source[h, :, r * span : (r + 1) * span], 0.0
            )

    for h in range(2):
        place(hwork, mine, h)
    for h in range(2):
        heat_copy(h).wait_recv()
        place(hgot, theirs, h)

    def average(v, before, beyond, node):
        return jnp.where(
            node == NODES - 1, 0.5 * (v + beyond), jnp.where(node == 0, 0.5 * (before + v), v)
        )

    def average_y(v, above, under):
        before = jnp.where(line_no == 0, above, pltpu.roll(v, 1, 0))
        beyond = jnp.where(line_no == lines - 1, under, pltpu.roll(v, lines - 1, 0))
        return average(v, before, beyond, node_y)

    for stage in range(3):
        def prepare(j, edges, stage=stage):
            west_edge, east_edge = edges
            for i in range(group):
                l = j * group + i
                if stage == 0:
                    value = heat_ref[at(l), :] - raw[at(l), :]
                else:
                    value = heat_ref[at(l), :] - wind(cur[at(l), :], l)
                raw[at(l), :] = value
                here = lane == l
                west_edge = jnp.where(here, pltpu.roll(value, l, 1), west_edge)
                east_edge = jnp.where(here, pltpu.roll(value, l + 1, 1), east_edge)
            return west_edge, east_edge

        nothing = jnp.zeros((lines, span), f32)
        west_edge, east_edge = lax.fori_loop(0, levels // group, prepare, (nothing, nothing))
        edgesnd[stage, 0] = west_edge
        edgesnd[stage, 1] = east_edge
        rowsnd[stage, 0] = raw[pl.ds(0, levels, stride=lines), :]
        rowsnd[stage, 1] = raw[pl.ds(lines - 1, levels, stride=lines), :]
        copies = []
        for n, device in enumerate(targets):
            if n < 6:
                source, sink = edgesnd.at[stage, 1 - n // 3], edgegot.at[stage, n]
            else:
                source, sink = rowsnd.at[stage, 7 - n], rowgot.at[stage, n - 6]
            copies.append(
                pltpu.make_async_remote_copy(
                    src_ref=source, dst_ref=sink, send_sem=halo_send.at[stage, n],
                    recv_sem=halo_recv.at[stage, n], device_id=device, device_id_type=MESH,
                )
            )
        for copy in copies:
            copy.start()
        for copy in copies:
            copy.wait_recv()
        beside = [
            average_y(
                edgegot[stage, 3 * side],
                edgegot[stage, 3 * side + 1, lines - 1 : lines, :],
                edgegot[stage, 3 * side + 2, 0:1, :],
            )
            for side in range(2)
        ]

        def finish(j, carry, stage=stage, beside=beside):
            for i in range(group):
                l = j * group + i
                value = average_y(
                    raw[at(l), :], rowgot[stage, 0, pl.ds(l, 1), :], rowgot[stage, 1, pl.ds(l, 1), :]
                )
                before = jnp.where(
                    lane == 0, pltpu.roll(beside[0], span - l, 1), pltpu.roll(value, 1, 1)
                )
                beyond = jnp.where(
                    lane == span - 1,
                    pltpu.roll(beside[1], span - 1 - l, 1),
                    pltpu.roll(value, span - 1, 1),
                )
                step = TIME_INCREMENT * average(value, before, beyond, node_x)
                start = temp_ref[at(l), :]
                if stage == 0:
                    cur[at(l), :] = start + step
                elif stage == 1:
                    cur[at(l), :] = 0.75 * start + 0.25 * (cur[at(l), :] + step)
                else:
                    adv_ref[at(l), :] = 1.0 / 3.0 * start + 2.0 / 3.0 * (cur[at(l), :] + step)
            return carry

        lax.fori_loop(0, levels // group, finish, 0)
        for copy in copies:
            copy.wait_send()
    for h in range(2):
        state_copy(h).wait_send()
        heat_copy(h).wait_send()


def solution(mesh):
    nx, ny = mesh.shape["gx"], mesh.shape["gy"]

    def local(
        atmospheric_constituents,
        thermal_ratio,
        flow_velocity,
        solar_elevation_factor,
        ground_reflectivity,
        sunlit_indicator,
        molecular_optics_lookup,
        condensate_optics_lookup,
    ):
        f32 = jnp.float32
        levels, lines, span = thermal_ratio.shape
        gtot = condensate_optics_lookup.shape[1]
        total = levels * lines
        wide = lines // 4 * span
        rows = FIELDS * levels + 8
        dma = pltpu.SemaphoreType.DMA
        heat, advected = pl.pallas_call(
            functools.partial(whole_kernel, nx, ny),
            out_shape=[jax.ShapeDtypeStruct((total, span), f32)] * 2,
            in_specs=[pl.BlockSpec(memory_space=pltpu.VMEM)] * 8,
            out_specs=[pl.BlockSpec(memory_space=pltpu.VMEM)] * 2,
            scratch_shapes=[
                pltpu.VMEM((2, rows, wide), f32),
                pltpu.VMEM((2, rows, wide), f32),
                pltpu.VMEM((2, wide // span, 8 * levels, span), f32),
                pltpu.VMEM((2, 3 * gtot, wide), f32),
                pltpu.VMEM((gtot, wide), f32),
                pltpu.VMEM((gtot, wide), f32),
                pltpu.VMEM((levels + 1, gtot, wide), f32),
                pltpu.VMEM((levels, gtot, wide), f32),
                pltpu.VMEM((levels, gtot, wide), f32),
                pltpu.VMEM((levels + 8, wide), f32),
                pltpu.VMEM((2, levels, wide), f32),
                pltpu.VMEM((2, levels, wide), f32),
                pltpu.VMEM((total, span), f32),
                pltpu.VMEM((total, span), f32),
                pltpu.VMEM((3, 2, levels, span), f32),
                pltpu.VMEM((3, 2, levels, span), f32),
                pltpu.VMEM((3, 2, lines, span), f32),
                pltpu.VMEM((3, 6, lines, span), f32),
                dma((2,)), dma((2,)), dma((2,)), dma((2,)), dma((3, 8)), dma((3, 8)),
            ],
            compiler_params=pltpu.CompilerParams(
                vmem_limit_bytes=58 * 2**20, collective_id=0, has_side_effects=True
            ),
            name="shortwave_advection",
        )(
            atmospheric_constituents.reshape(FIELDS * total, span),
            thermal_ratio.reshape(total, span),
            flow_velocity.reshape(2 * total, span),
            solar_elevation_factor,
            ground_reflectivity,
            sunlit_indicator,
            coef_matrix(molecular_optics_lookup, condensate_optics_lookup),
            condensate_optics_lookup[6][:, None],
        )
        return (heat.reshape(levels, lines, span), advected.reshape(levels, lines, span))

    in_specs = (
        P(None, None, "gy", "gx"),
        P(None, "gy", "gx"),
        P(None, None, "gy", "gx"),
        P("gy", "gx"),
        P("gy", "gx"),
        P("gy", "gx"),
        P(),
        P(),
    )
    out_specs = (P(None, "gy", "gx"), P(None, "gy", "gx"))
    return jax.shard_map(local, mesh=mesh, in_specs=in_specs, out_specs=out_specs, check_vma=False)
```

```python
import functools

import jax
import jax.numpy as jnp
import numpy as np
from jax import lax
from jax.experimental import pallas as pl
from jax.experimental.pallas import tpu as pltpu
from jax.sharding import PartitionSpec as P

NODES = 4
TIME_INCREMENT = 0.05
LOG2E = 1.4426950408889634
MESH = pl.DeviceIdType.MESH
FIELDS = 5
LANES = 8


def gll_derivative():
    points = np.array([-1.0, -1.0 / np.sqrt(5.0), 1.0 / np.sqrt(5.0), 1.0])
    legendre = 0.5 * (5.0 * points**3 - 3.0 * points)
    derivative = np.zeros((4, 4))
    for source in range(4):
        for target in range(4):
            if source != target:
                derivative[source, target] = legendre[source] / (
                    legendre[target] * (points[source] - points[target])
                )
    derivative[0, 0] = -3.0
    derivative[3, 3] = 3.0
    return derivative


def build_coefs(mol_ref, tab_ref, lhs_ref, w_ref, mols, waters):
    f32 = jnp.float32
    gtot, span = w_ref.shape[0], mols.shape[1]
    levels = mol_ref.shape[2]
    mols[...] = jnp.zeros_like(mols)
    for k in range(3):
        mols[k * gtot : (k + 1) * gtot, 0:levels] = mol_ref[k]
    waters[...] = jnp.zeros_like(waters)
    waters[0 : tab_ref.shape[0], 0:gtot] = tab_ref[...]
    table = waters[...].T
    w_ref[...] = table[0:gtot, 6:7]
    tile = 16
    lane = lax.broadcasted_iota(jnp.int32, (tile, span), 1)
    field = lane // LANES

    for i in range(gtot // tile):
        rows = slice(i * tile, (i + 1) * tile)
        lext, lalb, lasy, iext, ialb, iasy = (
            jnp.broadcast_to(table[rows, k : k + 1], (tile, span)) for k in range(6)
        )

        def water(liquid, ice):
            return jnp.where(field == 3, liquid, jnp.where(field == 4, ice, 0.0))

        fixed = [
            water(lext, iext),
            water(lext * (1 - lalb), iext * (1 - ialb)),
            water(lext * lalb * (1 - lasy), iext * ialb * (1 - iasy)),
        ]

        @pl.loop(0, lhs_ref.shape[0])
        def _(c, i=i, fixed=fixed):
            k0, k1, k2 = (
                pltpu.roll(
                    mols[pl.ds(k * gtot + i * tile, tile), :],
                    lax.rem(span + LANES * k - LANES * c, span),
                    1,
                )
                for k in range(3)
            )
            gas = jnp.where(field == 0, k0, jnp.where(field == 1, k1, 0.0))
            rayleigh = jnp.where(field == 2, k2, 0.0)
            sums = [2.0 * (fixed[0] + gas + rayleigh), fixed[1] + gas, fixed[2] + rayleigh]
            for n, value in enumerate(sums):
                high = value.astype(jnp.bfloat16).astype(f32)
                low = value - high
                wide = (
                    high
                    + pltpu.roll(high, FIELDS * LANES, 1)
                    + pltpu.roll(low, 2 * FIELDS * LANES, 1)
                )
                lhs_ref[c, pl.ds(n * gtot + i * tile, tile), :] = wide.astype(jnp.bfloat16)


def shortwave(
    prepare, base_ref, mask_ref, mu, ground, lhs_ref, w_ref, out_ref,
    mm, beam, src, a_all, p_all, o_all, flux,
):
    levels, gtot, n = p_all.shape
    blocks = gtot // 8
    chunks = levels // LANES
    f32 = jnp.float32
    nc = jnp.broadcast_to((-0.5 * LOG2E) / mu, (8, n))

    pieces = 3

    def right_side(l):
        return base_ref[lax.rem(l // LANES, 2)] * mask_ref[lax.rem(l, LANES)]

    def multiply(l, slot, rhs, piece):
        rows = pl.ds(gtot * piece, gtot)
        mm[slot, rows, :] = jnp.dot(
            lhs_ref[l // LANES, rows, :], rhs, preferred_element_type=f32
        )

    prepare(0)
    for piece in range(pieces):
        multiply(0, 0, right_side(0), piece)
    acc = jnp.zeros((8, n), f32)
    for i in range(blocks):
        sl = pl.ds(8 * i, 8)
        first = w_ref[sl, :] * mu
        beam[sl, :] = first
        src[sl, :] = jnp.zeros((8, n), f32)
        a_all[0, sl, :] = jnp.zeros((8, n), f32)
        acc = acc + first
    flux[0:1, :] = jnp.sum(acc, axis=0, keepdims=True)

    def down(l, slot):
        later = jnp.minimum(l + 1, levels - 1)
        rhs = right_side(later)
        acc = jnp.zeros((8, n), f32)
        for i in range(blocks):
            if i % 5 == 0:
                multiply(later, 1 - slot, rhs, i // 5)
            sl = pl.ds(8 * i, 8)
            t2 = mm[slot, sl, :]
            a = mm[slot, pl.ds(gtot + 8 * i, 8), :]
            b = mm[slot, pl.ds(2 * gtot + 8 * i, 8), :]
            bm = beam[sl, :]
            s = src[sl, :]
            alb = a_all[l, sl, :]
            c = a + b
            pr = a * c
            q = pr * lax.rsqrt(pr)
            t = jnp.tanh(q)
            x = a + c
            outer = q * (1.0 / t)
            inner = q * t
            rden = 1.0 / (x + outer + inner)
            refl = b * rden
            tran = (outer - inner) * rden
            bn = bm * jnp.exp2(t2 * nc)
            lost = bm - bn
            w = lost * (1.0 / t2)
            rb = w * b
            tb = lost - w * x
            inv = 1.0 / (1.0 - refl * alb)
            p = tran * inv
            o = (refl * s + rb) * inv
            a1 = refl + (tran * alb) * p
            s1 = tb + p * (s + alb * rb)
            p_all[l, sl, :] = p
            o_all[l, sl, :] = o
            a_all[l + 1, sl, :] = a1
            beam[sl, :] = bn
            src[sl, :] = s1
            acc = acc + (bn + s1)
        flux[pl.ds(l + 1, 1), :] = jnp.sum(acc, axis=0, keepdims=True)

    @pl.loop(0, chunks)
    def _(c):
        @pl.when(c + 1 < chunks)
        def _():
            prepare(c + 1)

        @pl.loop(0, LANES // 2)
        def _(h):
            l = c * LANES + 2 * h
            down(l, 0)
            down(l + 1, 1)

    ups = []
    acc = jnp.zeros((8, n), f32)
    for i in range(blocks):
        sl = pl.ds(8 * i, 8)
        alb = a_all[levels, sl, :]
        up = ground * (src[sl, :] + beam[sl, :]) * (1.0 / (1.0 - ground * alb))
        ups.append(up)
        acc = acc + (1.0 - alb) * up
    last = pl.ds(levels, 1)
    flux[last, :] = flux[last, :] - jnp.sum(acc, axis=0, keepdims=True)

    def upward(k, ups):
        l = levels - 1 - k
        acc = jnp.zeros((8, n), f32)
        out = []
        for i in range(blocks):
            sl = pl.ds(8 * i, 8)
            up = p_all[l, sl, :] * ups[i] + o_all[l, sl, :]
            acc = acc + (1.0 - a_all[l, sl, :]) * up
            out.append(up)
        row = pl.ds(l, 1)
        flux[row, :] = flux[row, :] - jnp.sum(acc, axis=0, keepdims=True)
        return tuple(out)

    lax.fori_loop(0, levels, upward, tuple(ups))
    out_ref[...] = (levels / gtot) * (flux[0:levels, :] - flux[1 : levels + 1, :])


def whole_kernel(
    nx, ny, state_ref, temp_ref, flow_ref, mu_ref, ground_ref, day_ref, mol_ref, tab_ref,
    heat_ref, adv_ref,
    snd, got, sfcsnd, sfcgot, base, mask, lhs_ref, w_ref, mols, waters, mm, beam, src, a_all, p_all, o_all, flux, hwork, hgot,
    raw, cur, rowsnd, rowgot, edgesnd, edgegot,
    state_send, state_recv, sfc_send, sfc_recv, heat_send, heat_recv, halo_send, halo_recv,
):
    f32 = jnp.float32
    gx, gy = lax.axis_index("gx"), lax.axis_index("gy")
    lines, span = mu_ref.shape
    total = temp_ref.shape[0]
    levels = total // lines
    half = lines // 2
    pair = half // 2
    east, west = lax.rem(gx + 1, nx), lax.rem(gx + nx - 1, nx)
    south, north = lax.rem(gy + 1, ny), lax.rem(gy + ny - 1, ny)
    far = lax.rem(gx + nx // 2, nx)
    mine = jnp.where(gx < nx // 2, 0, half)
    theirs = half - mine

    targets = [
        (east, gy), (east, south), (east, north),
        (west, gy), (west, south), (west, north),
        (gx, south), (gx, north),
    ]
    barrier = pltpu.get_barrier_semaphore()
    for device in targets + [(far, gy)]:
        pl.semaphore_signal(barrier, inc=1, device_id=device, device_id_type=MESH)
    pl.semaphore_wait(barrier, len(targets) + 1)

    chunks = levels // LANES

    def products(line, c):
        def line_of(ref, k):
            return ref[pl.ds(k * total + c * (LANES * lines) + line, LANES, stride=lines), :]

        temper = line_of(temp_ref, 0)
        thick = line_of(state_ref, 2)
        weighted = thick * temper * temper
        return [
            weighted * line_of(state_ref, 0),
            weighted * line_of(state_ref, 1),
            thick,
            line_of(state_ref, 3),
            line_of(state_ref, 4),
        ]

    def state_copy(h, c):
        return pltpu.make_async_remote_copy(
            src_ref=snd.at[h, c], dst_ref=got.at[h, c], send_sem=state_send.at[h, c],
            recv_sem=state_recv.at[h, c], device_id=(far, gy), device_id_type=MESH,
        )

    surface_copy = pltpu.make_async_remote_copy(
        src_ref=sfcsnd, dst_ref=sfcgot, send_sem=sfc_send, recv_sem=sfc_recv,
        device_id=(far, gy), device_id_type=MESH,
    )

    def heat_copy(h):
        return pltpu.make_async_remote_copy(
            src_ref=hwork.at[h], dst_ref=hgot.at[h], send_sem=heat_send.at[h],
            recv_sem=heat_recv.at[h], device_id=(far, gy), device_id_type=MESH,
        )

    for n in range(half):
        line = pl.ds(theirs + n, 1)
        sfcsnd[n : n + 1, :] = mu_ref[line, :]
        sfcsnd[half + n : half + n + 1, :] = ground_ref[line, :]
    surface_copy.start()

    def send_state(h, c):
        for r in range(pair):
            for k, value in enumerate(products(theirs + pair * h + r, c)):
                snd[h, c, k * LANES : (k + 1) * LANES, r * span : (r + 1) * span] = value
        state_copy(h, c).start()

    @pl.loop(0, chunks)
    def _(c):
        send_state(0, c)

    build_coefs(mol_ref, tab_ref, lhs_ref, w_ref, mols, waters)
    row_no = lax.broadcasted_iota(jnp.int32, mask.shape[1:], 0)
    for j in range(LANES):
        mask[j] = jnp.where(lax.rem(row_no, LANES) == j, 1.0, 0.0).astype(jnp.bfloat16)

    dref = gll_derivative()
    lane = lax.broadcasted_iota(jnp.int32, (lines, span), 1)
    line_no = lax.broadcasted_iota(jnp.int32, (lines, span), 0)
    node_x, node_y = lane % NODES, line_no % NODES

    def taps(node):
        out = []
        for k in range(1 - NODES, NODES):
            coef = jnp.zeros((lines, span), f32)
            for i in range(NODES):
                if 0 <= i + k < NODES and dref[i, i + k] != 0.0:
                    coef = jnp.where(node == i, float(dref[i, i + k]), coef)
            out.append((k, coef))
        return out

    taps_x, taps_y = taps(node_x), taps(node_y)

    def slope(v, axis, size, table):
        out = None
        for k, coef in table:
            moved = v if k == 0 else pltpu.roll(v, (-k) % size, axis)
            out = coef * moved if out is None else out + coef * moved
        return out

    def at(l):
        return pl.ds(pl.multiple_of(l * lines, lines), lines)

    def wind(v, l):
        return flow_ref[at(l), :] * slope(v, 1, span, taps_x) + flow_ref[
            at(levels + l), :
        ] * slope(v, 0, lines, taps_y)

    group = 8

    @pl.loop(0, levels // group)
    def _(j):
        for i in range(group):
            l = j * group + i
            raw[at(l), :] = wind(temp_ref[at(l), :], l)

    surface_copy.wait_recv()
    for h in range(2):
        mus, grounds = [], []
        for r in range(pair):
            line = pl.ds(mine + pair * h + r, 1)
            own = day_ref[line, :] == 1
            n = pair * h + r
            mus.append(jnp.where(own, mu_ref[line, :], sfcgot[n : n + 1, :]))
            grounds.append(
                jnp.where(own, ground_ref[line, :], sfcgot[half + n : half + n + 1, :])
            )

        def prepare(c, h=h):
            state_copy(h, c).wait_recv()
            if h == 0:
                send_state(1, c)
            highs, lows = [[] for _ in range(FIELDS)], [[] for _ in range(FIELDS)]
            for r in range(pair):
                line = mine + pair * h + r
                own = day_ref[pl.ds(line, 1), :] == 1
                for k, value in enumerate(products(line, c)):
                    other = got[h, c, k * LANES : (k + 1) * LANES, r * span : (r + 1) * span]
                    value = jnp.where(own, value, other)
                    high = value.astype(jnp.bfloat16).astype(f32)
                    highs[k].append(high)
                    lows[k].append(value - high)
            highs = [jnp.concatenate(v, axis=1) for v in highs]
            lows = [jnp.concatenate(v, axis=1) for v in lows]
            parts = highs + lows + highs + [jnp.zeros_like(highs[0])]
            base[lax.rem(c, 2)] = jnp.concatenate(parts, axis=0).astype(jnp.bfloat16)

        shortwave(
            prepare, base, mask, jnp.concatenate(mus, axis=1), jnp.concatenate(grounds, axis=1),
            lhs_ref, w_ref, hwork.at[h], mm, beam, src, a_all, p_all, o_all, flux,
        )
        heat_copy(h).start()

    def place(source, first, h):
        for r in range(pair):
            line = first + pair * h + r
            own = day_ref[pl.ds(line, 1), :] == 1
            heat_ref[pl.ds(line, levels, stride=lines), :] = jnp.where(
                own, source[h, :, r * span : (r + 1) * span], 0.0
            )

    for h in range(2):
        place(hwork, mine, h)
    for h in range(2):
        heat_copy(h).wait_recv()
        place(hgot, theirs, h)

    def average(v, before, beyond, node):
        return jnp.where(
            node == NODES - 1, 0.5 * (v + beyond), jnp.where(node == 0, 0.5 * (before + v), v)
        )

    def average_y(v, above, under):
        before = jnp.where(line_no == 0, above, pltpu.roll(v, 1, 0))
        beyond = jnp.where(line_no == lines - 1, under, pltpu.roll(v, lines - 1, 0))
        return average(v, before, beyond, node_y)

    for stage in range(3):
        def prepare(j, edges, stage=stage):
            west_edge, east_edge = edges
            for i in range(group):
                l = j * group + i
                if stage == 0:
                    value = heat_ref[at(l), :] - raw[at(l), :]
                else:
                    value = heat_ref[at(l), :] - wind(cur[at(l), :], l)
                raw[at(l), :] = value
                here = lane == l
                west_edge = jnp.where(here, pltpu.roll(value, l, 1), west_edge)
                east_edge = jnp.where(here, pltpu.roll(value, l + 1, 1), east_edge)
            return west_edge, east_edge

        nothing = jnp.zeros((lines, span), f32)
        west_edge, east_edge = lax.fori_loop(0, levels // group, prepare, (nothing, nothing))
        edgesnd[stage, 0] = west_edge
        edgesnd[stage, 1] = east_edge
        rowsnd[stage, 0] = raw[pl.ds(0, levels, stride=lines), :]
        rowsnd[stage, 1] = raw[pl.ds(lines - 1, levels, stride=lines), :]
        copies = []
        for n, device in enumerate(targets):
            if n < 6:
                source, sink = edgesnd.at[stage, 1 - n // 3], edgegot.at[stage, n]
            else:
                source, sink = rowsnd.at[stage, 7 - n], rowgot.at[stage, n - 6]
            copies.append(
                pltpu.make_async_remote_copy(
                    src_ref=source, dst_ref=sink, send_sem=halo_send.at[stage, n],
                    recv_sem=halo_recv.at[stage, n], device_id=device, device_id_type=MESH,
                )
            )
        for copy in copies:
            copy.start()
        for copy in copies:
            copy.wait_recv()
        beside = [
            average_y(
                edgegot[stage, 3 * side],
                edgegot[stage, 3 * side + 1, lines - 1 : lines, :],
                edgegot[stage, 3 * side + 2, 0:1, :],
            )
            for side in range(2)
        ]

        def finish(j, carry, stage=stage, beside=beside):
            for i in range(group):
                l = j * group + i
                value = average_y(
                    raw[at(l), :], rowgot[stage, 0, pl.ds(l, 1), :], rowgot[stage, 1, pl.ds(l, 1), :]
                )
                before = jnp.where(
                    lane == 0, pltpu.roll(beside[0], span - l, 1), pltpu.roll(value, 1, 1)
                )
                beyond = jnp.where(
                    lane == span - 1,
                    pltpu.roll(beside[1], span - 1 - l, 1),
                    pltpu.roll(value, span - 1, 1),
                )
                step = TIME_INCREMENT * average(value, before, beyond, node_x)
                start = temp_ref[at(l), :]
                if stage == 0:
                    cur[at(l), :] = start + step
                elif stage == 1:
                    cur[at(l), :] = 0.75 * start + 0.25 * (cur[at(l), :] + step)
                else:
                    adv_ref[at(l), :] = 1.0 / 3.0 * start + 2.0 / 3.0 * (cur[at(l), :] + step)
            return carry

        lax.fori_loop(0, levels // group, finish, 0)
        for copy in copies:
            copy.wait_send()
    surface_copy.wait_send()
    for h in range(2):
        heat_copy(h).wait_send()

        @pl.loop(0, chunks)
        def _(c, h=h):
            state_copy(h, c).wait_send()


def finish_kernel(heat_ref, adv_ref, heat_out, adv_out):
    heat_out[...] = heat_ref[...]
    adv_out[...] = adv_ref[...]


def solution(mesh):
    nx, ny = mesh.shape["gx"], mesh.shape["gy"]

    def local(
        atmospheric_constituents,
        thermal_ratio,
        flow_velocity,
        solar_elevation_factor,
        ground_reflectivity,
        sunlit_indicator,
        molecular_optics_lookup,
        condensate_optics_lookup,
    ):
        f32 = jnp.float32
        levels, lines, span = thermal_ratio.shape
        gtot = condensate_optics_lookup.shape[1]
        total = levels * lines
        wide = lines // 4 * span
        chunks = levels // LANES
        dma = pltpu.SemaphoreType.DMA
        heat, advected = pl.pallas_call(
            functools.partial(whole_kernel, nx, ny),
            out_shape=[jax.ShapeDtypeStruct((total, span), f32)] * 2,
            in_specs=[pl.BlockSpec(memory_space=pltpu.VMEM)] * 8,
            out_specs=[pl.BlockSpec(memory_space=pltpu.VMEM)] * 2,
            scratch_shapes=[
                pltpu.VMEM((2, chunks, FIELDS * LANES, wide), f32),
                pltpu.VMEM((2, chunks, FIELDS * LANES, wide), f32),
                pltpu.VMEM((lines, span), f32),
                pltpu.VMEM((lines, span), f32),
                pltpu.VMEM((2, 128, wide), jnp.bfloat16),
                pltpu.VMEM((LANES, 128, wide), jnp.bfloat16),
                pltpu.VMEM((chunks, 3 * gtot, 128), jnp.bfloat16),
                pltpu.VMEM((gtot, 1), f32),
                pltpu.VMEM((3 * gtot, 128), f32),
                pltpu.VMEM((8, 128), f32),
                pltpu.VMEM((2, 3 * gtot, wide), f32),
                pltpu.VMEM((gtot, wide), f32),
                pltpu.VMEM((gtot, wide), f32),
                pltpu.VMEM((levels + 1, gtot, wide), f32),
                pltpu.VMEM((levels, gtot, wide), f32),
                pltpu.VMEM((levels, gtot, wide), f32),
                pltpu.VMEM((levels + 8, wide), f32),
                pltpu.VMEM((2, levels, wide), f32),
                pltpu.VMEM((2, levels, wide), f32),
                pltpu.VMEM((total, span), f32),
                pltpu.VMEM((total, span), f32),
                pltpu.VMEM((3, 2, levels, span), f32),
                pltpu.VMEM((3, 2, levels, span), f32),
                pltpu.VMEM((3, 2, lines, span), f32),
                pltpu.VMEM((3, 6, lines, span), f32),
                dma((2, chunks)), dma((2, chunks)), dma(()), dma(()), dma((2,)), dma((2,)),
                dma((3, 8)), dma((3, 8)),
            ],
            compiler_params=pltpu.CompilerParams(
                vmem_limit_bytes=58 * 2**20, collective_id=0, has_side_effects=True
            ),
            name="shortwave_advection",
        )(
            atmospheric_constituents.reshape(FIELDS * total, span),
            thermal_ratio.reshape(total, span),
            flow_velocity.reshape(2 * total, span),
            solar_elevation_factor,
            ground_reflectivity,
            sunlit_indicator,
            molecular_optics_lookup,
            condensate_optics_lookup,
        )
        spec = pl.BlockSpec((total // 3, span), lambda i: (i, 0))
        heat, advected = pl.pallas_call(
            finish_kernel,
            grid=(3,),
            out_shape=[jax.ShapeDtypeStruct((total, span), f32)] * 2,
            in_specs=[spec] * 2,
            out_specs=[spec] * 2,
            name="results",
        )(heat, advected)
        return (heat.reshape(levels, lines, span), advected.reshape(levels, lines, span))

    in_specs = (
        P(None, None, "gy", "gx"),
        P(None, "gy", "gx"),
        P(None, None, "gy", "gx"),
        P("gy", "gx"),
        P("gy", "gx"),
        P("gy", "gx"),
        P(),
        P(),
    )
    out_specs = (P(None, "gy", "gx"), P(None, "gy", "gx"))
    return jax.shard_map(local, mesh=mesh, in_specs=in_specs, out_specs=out_specs, check_vma=False)
```

```python
import functools

import jax
import jax.numpy as jnp
import numpy as np
from jax import lax
from jax.experimental import pallas as pl
from jax.experimental.pallas import tpu as pltpu
from jax.sharding import PartitionSpec as P

NODES = 4
TIME_INCREMENT = 0.05
LOG2E = 1.4426950408889634
MESH = pl.DeviceIdType.MESH
FIELDS = 5
LANES = 8
PARTS = 3


def gll_derivative():
    points = np.array([-1.0, -1.0 / np.sqrt(5.0), 1.0 / np.sqrt(5.0), 1.0])
    legendre = 0.5 * (5.0 * points**3 - 3.0 * points)
    derivative = np.zeros((4, 4))
    for source in range(4):
        for target in range(4):
            if source != target:
                derivative[source, target] = legendre[source] / (
                    legendre[target] * (points[source] - points[target])
                )
    derivative[0, 0] = -3.0
    derivative[3, 3] = 3.0
    return derivative


def build_coefs(mol_ref, tab_ref, lhs_ref, w_ref, mols, waters, flip):
    f32 = jnp.float32
    gtot, span = w_ref.shape[0], mols.shape[1]
    levels = mol_ref.shape[1]
    for k in range(3):
        flip[...] = jnp.zeros_like(flip)
        flip[0:levels, 0:gtot] = mol_ref[k]
        mols[k * gtot : (k + 1) * gtot, :] = flip[...].T[0:gtot, :]
    waters[...] = jnp.zeros_like(waters)
    waters[0 : tab_ref.shape[0], 0:gtot] = tab_ref[...]
    table = waters[...].T
    w_ref[...] = table[0:gtot, 6:7]
    tile = 16
    lane = lax.broadcasted_iota(jnp.int32, (tile, span), 1)
    field = lane // LANES

    for i in range(gtot // tile):
        rows = slice(i * tile, (i + 1) * tile)
        lext, lalb, lasy, iext, ialb, iasy = (
            jnp.broadcast_to(table[rows, k : k + 1], (tile, span)) for k in range(6)
        )

        def water(liquid, ice):
            return jnp.where(field == 3, liquid, jnp.where(field == 4, ice, 0.0))

        fixed = [
            water(lext, iext),
            water(lext * (1 - lalb), iext * (1 - ialb)),
            water(lext * lalb * (1 - lasy), iext * ialb * (1 - iasy)),
        ]

        @pl.loop(0, lhs_ref.shape[0])
        def _(c, i=i, fixed=fixed):
            k0, k1, k2 = (
                pltpu.roll(
                    mols[pl.ds(k * gtot + i * tile, tile), :],
                    lax.rem(span + LANES * k - LANES * c, span),
                    1,
                )
                for k in range(3)
            )
            gas = jnp.where(field == 0, k0, jnp.where(field == 1, k1, 0.0))
            rayleigh = jnp.where(field == 2, k2, 0.0)
            sums = [2.0 * (fixed[0] + gas + rayleigh), fixed[1] + gas, fixed[2] + rayleigh]
            for n, value in enumerate(sums):
                high = value.astype(jnp.bfloat16).astype(f32)
                low = value - high
                wide = (
                    high
                    + pltpu.roll(high, FIELDS * LANES, 1)
                    + pltpu.roll(low, 2 * FIELDS * LANES, 1)
                )
                lhs_ref[c, pl.ds(n * gtot + i * tile, tile), :] = wide.astype(jnp.bfloat16)


def shortwave(
    prepare, base_ref, mask_ref, mu, ground, lhs_ref, w_ref, out_ref,
    mm, beam, src, a_all, p_all, o_all, flux,
):
    levels, gtot, n = p_all.shape
    blocks = gtot // 8
    chunks = levels // LANES
    f32 = jnp.float32
    nc = jnp.broadcast_to((-0.5 * LOG2E) / mu, (8, n))

    pieces = 3

    def right_side(l):
        return base_ref[lax.rem(l // LANES, 2)] * mask_ref[lax.rem(l, LANES)]

    def multiply(l, slot, rhs, piece):
        rows = pl.ds(gtot * piece, gtot)
        mm[slot, rows, :] = jnp.dot(
            lhs_ref[l // LANES, rows, :], rhs, preferred_element_type=f32
        )

    prepare(0)
    for piece in range(pieces):
        multiply(0, 0, right_side(0), piece)
    acc = jnp.zeros((8, n), f32)
    for i in range(blocks):
        sl = pl.ds(8 * i, 8)
        first = w_ref[sl, :] * mu
        beam[sl, :] = first
        src[sl, :] = jnp.zeros((8, n), f32)
        a_all[0, sl, :] = jnp.zeros((8, n), f32)
        acc = acc + first
    flux[0:1, :] = jnp.sum(acc, axis=0, keepdims=True)

    def down(l, slot):
        later = jnp.minimum(l + 1, levels - 1)
        rhs = right_side(later)
        acc = jnp.zeros((8, n), f32)
        for i in range(blocks):
            if i % 5 == 0:
                multiply(later, 1 - slot, rhs, i // 5)
            sl = pl.ds(8 * i, 8)
            t2 = mm[slot, sl, :]
            a = mm[slot, pl.ds(gtot + 8 * i, 8), :]
            b = mm[slot, pl.ds(2 * gtot + 8 * i, 8), :]
            bm = beam[sl, :]
            s = src[sl, :]
            alb = a_all[l, sl, :]
            c = a + b
            pr = a * c
            q = pr * lax.rsqrt(pr)
            t = jnp.tanh(q)
            x = a + c
            outer = q * (1.0 / t)
            inner = q * t
            rden = 1.0 / (x + outer + inner)
            refl = b * rden
            tran = (outer - inner) * rden
            bn = bm * jnp.exp2(t2 * nc)
            lost = bm - bn
            w = lost * (1.0 / t2)
            rb = w * b
            tb = lost - w * x
            inv = 1.0 / (1.0 - refl * alb)
            p = tran * inv
            o = (refl * s + rb) * inv
            a1 = refl + (tran * alb) * p
            s1 = tb + p * (s + alb * rb)
            p_all[l, sl, :] = p
            o_all[l, sl, :] = o
            a_all[l + 1, sl, :] = a1
            beam[sl, :] = bn
            src[sl, :] = s1
            acc = acc + (bn + s1)
        flux[pl.ds(l + 1, 1), :] = jnp.sum(acc, axis=0, keepdims=True)

    @pl.loop(0, chunks)
    def _(c):
        @pl.when(c + 1 < chunks)
        def _():
            prepare(c + 1)

        @pl.loop(0, LANES // 2)
        def _(h):
            l = c * LANES + 2 * h
            down(l, 0)
            down(l + 1, 1)

    ups = []
    acc = jnp.zeros((8, n), f32)
    for i in range(blocks):
        sl = pl.ds(8 * i, 8)
        alb = a_all[levels, sl, :]
        up = ground * (src[sl, :] + beam[sl, :]) * (1.0 / (1.0 - ground * alb))
        ups.append(up)
        acc = acc + (1.0 - alb) * up
    last = pl.ds(levels, 1)
    flux[last, :] = flux[last, :] - jnp.sum(acc, axis=0, keepdims=True)

    def upward(k, ups):
        l = levels - 1 - k
        acc = jnp.zeros((8, n), f32)
        out = []
        for i in range(blocks):
            sl = pl.ds(8 * i, 8)
            up = p_all[l, sl, :] * ups[i] + o_all[l, sl, :]
            acc = acc + (1.0 - a_all[l, sl, :]) * up
            out.append(up)
        row = pl.ds(l, 1)
        flux[row, :] = flux[row, :] - jnp.sum(acc, axis=0, keepdims=True)
        return tuple(out)

    lax.fori_loop(0, levels, upward, tuple(ups))
    out_ref[...] = (levels / gtot) * (flux[0:levels, :] - flux[1 : levels + 1, :])


def whole_kernel(
    nx, ny, state_ref, temp_ref, flow_ref, mu_ref, ground_ref, day_ref, mol_ref, tab_ref,
    heat_ref, adv_ref,
    snd, got, sfcsnd, sfcgot, base, mask, lhs_ref, w_ref, mols, waters, flip, mm, beam, src, a_all, p_all, o_all, flux, hwork, hgot,
    raw, cur, rowsnd, rowgot, edgesnd, edgegot,
    state_send, state_recv, sfc_send, sfc_recv, heat_send, heat_recv, halo_send, halo_recv,
):
    f32 = jnp.float32
    gx, gy = lax.axis_index("gx"), lax.axis_index("gy")
    lines, span = mu_ref.shape
    total = temp_ref.shape[0]
    levels = total // lines
    half = lines // 2
    pair = half // 2
    east, west = lax.rem(gx + 1, nx), lax.rem(gx + nx - 1, nx)
    south, north = lax.rem(gy + 1, ny), lax.rem(gy + ny - 1, ny)
    far = lax.rem(gx + nx // 2, nx)
    mine = jnp.where(gx < nx // 2, 0, half)
    theirs = half - mine

    targets = [
        (east, gy), (east, south), (east, north),
        (west, gy), (west, south), (west, north),
        (gx, south), (gx, north),
    ]
    barrier = pltpu.get_barrier_semaphore()
    for device in targets + [(far, gy)]:
        pl.semaphore_signal(barrier, inc=1, device_id=device, device_id_type=MESH)
    pl.semaphore_wait(barrier, len(targets) + 1)

    chunks = levels // LANES

    def products(line, c):
        def line_of(ref, k):
            return ref[pl.ds(k * total + c * (LANES * lines) + line, LANES, stride=lines), :]

        temper = line_of(temp_ref, 0)
        thick = line_of(state_ref, 2)
        weighted = thick * temper * temper
        return [
            weighted * line_of(state_ref, 0),
            weighted * line_of(state_ref, 1),
            thick,
            line_of(state_ref, 3),
            line_of(state_ref, 4),
        ]

    def state_copy(h, c):
        return pltpu.make_async_remote_copy(
            src_ref=snd.at[h, c], dst_ref=got.at[h, c], send_sem=state_send.at[h, c],
            recv_sem=state_recv.at[h, c], device_id=(far, gy), device_id_type=MESH,
        )

    surface_copy = pltpu.make_async_remote_copy(
        src_ref=sfcsnd, dst_ref=sfcgot, send_sem=sfc_send, recv_sem=sfc_recv,
        device_id=(far, gy), device_id_type=MESH,
    )

    def heat_copy(h):
        return pltpu.make_async_remote_copy(
            src_ref=hwork.at[h], dst_ref=hgot.at[h], send_sem=heat_send.at[h],
            recv_sem=heat_recv.at[h], device_id=(far, gy), device_id_type=MESH,
        )

    for n in range(half):
        line = pl.ds(theirs + n, 1)
        sfcsnd[n : n + 1, :] = mu_ref[line, :]
        sfcsnd[half + n : half + n + 1, :] = ground_ref[line, :]
    surface_copy.start()

    def send_state(h, c):
        for r in range(pair):
            for k, value in enumerate(products(theirs + pair * h + r, c)):
                snd[h, c, k * LANES : (k + 1) * LANES, r * span : (r + 1) * span] = value
        state_copy(h, c).start()

    @pl.loop(0, chunks)
    def _(c):
        send_state(0, c)

    build_coefs(mol_ref, tab_ref, lhs_ref, w_ref, mols, waters, flip)
    row_no = lax.broadcasted_iota(jnp.int32, mask.shape[1:], 0)
    for j in range(LANES):
        mask[j] = jnp.where(lax.rem(row_no, LANES) == j, 1.0, 0.0).astype(jnp.bfloat16)

    dref = gll_derivative()
    lane = lax.broadcasted_iota(jnp.int32, (lines, span), 1)
    line_no = lax.broadcasted_iota(jnp.int32, (lines, span), 0)
    node_x, node_y = lane % NODES, line_no % NODES

    def taps(node):
        out = []
        for k in range(1 - NODES, NODES):
            coef = jnp.zeros((lines, span), f32)
            for i in range(NODES):
                if 0 <= i + k < NODES and dref[i, i + k] != 0.0:
                    coef = jnp.where(node == i, float(dref[i, i + k]), coef)
            out.append((k, coef))
        return out

    taps_x, taps_y = taps(node_x), taps(node_y)

    def slope(v, axis, size, table):
        out = None
        for k, coef in table:
            moved = v if k == 0 else pltpu.roll(v, (-k) % size, axis)
            out = coef * moved if out is None else out + coef * moved
        return out

    def at(l):
        return pl.ds(pl.multiple_of(l * lines, lines), lines)

    def wind(v, l):
        return flow_ref[at(l), :] * slope(v, 1, span, taps_x) + flow_ref[
            at(levels + l), :
        ] * slope(v, 0, lines, taps_y)

    group = 8

    @pl.loop(0, levels // group)
    def _(j):
        for i in range(group):
            l = j * group + i
            raw[at(l), :] = wind(temp_ref[at(l), :], l)

    surface_copy.wait_recv()
    for h in range(2):
        mus, grounds = [], []
        for r in range(pair):
            line = pl.ds(mine + pair * h + r, 1)
            own = day_ref[line, :] == 1
            n = pair * h + r
            mus.append(jnp.where(own, mu_ref[line, :], sfcgot[n : n + 1, :]))
            grounds.append(
                jnp.where(own, ground_ref[line, :], sfcgot[half + n : half + n + 1, :])
            )

        def prepare(c, h=h):
            state_copy(h, c).wait_recv()
            if h == 0:
                send_state(1, c)
            highs, lows = [[] for _ in range(FIELDS)], [[] for _ in range(FIELDS)]
            for r in range(pair):
                line = mine + pair * h + r
                own = day_ref[pl.ds(line, 1), :] == 1
                for k, value in enumerate(products(line, c)):
                    other = got[h, c, k * LANES : (k + 1) * LANES, r * span : (r + 1) * span]
                    value = jnp.where(own, value, other)
                    high = value.astype(jnp.bfloat16).astype(f32)
                    highs[k].append(high)
                    lows[k].append(value - high)
            highs = [jnp.concatenate(v, axis=1) for v in highs]
            lows = [jnp.concatenate(v, axis=1) for v in lows]
            parts = highs + lows + highs + [jnp.zeros_like(highs[0])]
            base[lax.rem(c, 2)] = jnp.concatenate(parts, axis=0).astype(jnp.bfloat16)

        shortwave(
            prepare, base, mask, jnp.concatenate(mus, axis=1), jnp.concatenate(grounds, axis=1),
            lhs_ref, w_ref, hwork.at[h], mm, beam, src, a_all, p_all, o_all, flux,
        )
        heat_copy(h).start()

    def place(source, first, h):
        for r in range(pair):
            line = first + pair * h + r
            own = day_ref[pl.ds(line, 1), :] == 1
            heat_ref[pl.ds(line, levels, stride=lines), :] = jnp.where(
                own, source[h, :, r * span : (r + 1) * span], 0.0
            )

    for h in range(2):
        place(hwork, mine, h)
    for h in range(2):
        heat_copy(h).wait_recv()
        place(hgot, theirs, h)

    def average(v, before, beyond, node):
        return jnp.where(
            node == NODES - 1, 0.5 * (v + beyond), jnp.where(node == 0, 0.5 * (before + v), v)
        )

    def average_y(v, above, under):
        before = jnp.where(line_no == 0, above, pltpu.roll(v, 1, 0))
        beyond = jnp.where(line_no == lines - 1, under, pltpu.roll(v, lines - 1, 0))
        return average(v, before, beyond, node_y)

    parts = rowsnd.shape[1]
    depth = levels // parts
    steps = depth // group

    def halo_copies(stage, g):
        copies = []
        for n, device in enumerate(targets):
            if n < 6:
                source, sink = edgesnd.at[stage, g, 1 - n // 3], edgegot.at[stage, g, n]
            else:
                source, sink = rowsnd.at[stage, g, 7 - n], rowgot.at[stage, g, n - 6]
            copies.append(
                pltpu.make_async_remote_copy(
                    src_ref=source, dst_ref=sink, send_sem=halo_send.at[stage, g, n],
                    recv_sem=halo_recv.at[stage, g, n], device_id=device, device_id_type=MESH,
                )
            )
        return copies

    def emit(stage, g):
        def prepare(j, edges):
            west_edge, east_edge = edges
            for i in range(group):
                l = g * depth + j * group + i
                if stage == 0:
                    value = heat_ref[at(l), :] - raw[at(l), :]
                else:
                    value = heat_ref[at(l), :] - wind(cur[at(l), :], l)
                raw[at(l), :] = value
                here = lane == l
                west_edge = jnp.where(here, pltpu.roll(value, l, 1), west_edge)
                east_edge = jnp.where(here, pltpu.roll(value, l + 1, 1), east_edge)
            return west_edge, east_edge

        nothing = jnp.zeros((lines, span), f32)
        west_edge, east_edge = lax.fori_loop(0, steps, prepare, (nothing, nothing))
        edgesnd[stage, g, 0] = west_edge
        edgesnd[stage, g, 1] = east_edge
        for side, line in enumerate((0, lines - 1)):
            rowsnd[stage, g, side] = raw[pl.ds(g * depth * lines + line, depth, stride=lines), :]
        for copy in halo_copies(stage, g):
            copy.start()

    def absorb(stage, g):
        for copy in halo_copies(stage, g):
            copy.wait_recv()
        beside = [
            average_y(
                edgegot[stage, g, 3 * side],
                edgegot[stage, g, 3 * side + 1, lines - 1 : lines, :],
                edgegot[stage, g, 3 * side + 2, 0:1, :],
            )
            for side in range(2)
        ]

        def finish(j, carry):
            for i in range(group):
                k = j * group + i
                l = g * depth + k
                value = average_y(
                    raw[at(l), :],
                    rowgot[stage, g, 0, pl.ds(k, 1), :],
                    rowgot[stage, g, 1, pl.ds(k, 1), :],
                )
                before = jnp.where(
                    lane == 0, pltpu.roll(beside[0], span - l, 1), pltpu.roll(value, 1, 1)
                )
                beyond = jnp.where(
                    lane == span - 1,
                    pltpu.roll(beside[1], span - 1 - l, 1),
                    pltpu.roll(value, span - 1, 1),
                )
                step = TIME_INCREMENT * average(value, before, beyond, node_x)
                start = temp_ref[at(l), :]
                if stage == 0:
                    cur[at(l), :] = start + step
                elif stage == 1:
                    cur[at(l), :] = 0.75 * start + 0.25 * (cur[at(l), :] + step)
                else:
                    adv_ref[at(l), :] = 1.0 / 3.0 * start + 2.0 / 3.0 * (cur[at(l), :] + step)
            return carry

        lax.fori_loop(0, steps, finish, 0)

    for g in range(parts):
        emit(0, g)
    for stage in range(3):
        for g in range(parts):
            absorb(stage, g)
            if stage < 2:
                emit(stage + 1, g)
    for stage in range(3):
        for g in range(parts):
            for copy in halo_copies(stage, g):
                copy.wait_send()
    surface_copy.wait_send()
    for h in range(2):
        heat_copy(h).wait_send()

        @pl.loop(0, chunks)
        def _(c, h=h):
            state_copy(h, c).wait_send()


def finish_kernel(heat_ref, adv_ref, heat_out, adv_out, hold, sems):
    rows = hold.shape[2]
    stages = []
    for n, (source, sink) in enumerate(((heat_ref, heat_out), (adv_ref, adv_out))):
        for part in range(hold.shape[1]):
            here = pl.ds(part * rows, rows)
            keep = hold.at[n, part]
            stages.append(
                (
                    pltpu.make_async_copy(source.at[here], keep, sems.at[0, n, part]),
                    pltpu.make_async_copy(keep, sink.at[here], sems.at[1, n, part]),
                )
            )
    for first, _ in stages:
        first.start()
    for first, second in stages:
        first.wait()
        second.start()
    for _, second in stages:
        second.wait()


def solution(mesh):
    nx, ny = mesh.shape["gx"], mesh.shape["gy"]

    def local(
        atmospheric_constituents,
        thermal_ratio,
        flow_velocity,
        solar_elevation_factor,
        ground_reflectivity,
        sunlit_indicator,
        molecular_optics_lookup,
        condensate_optics_lookup,
    ):
        f32 = jnp.float32
        levels, lines, span = thermal_ratio.shape
        gtot = condensate_optics_lookup.shape[1]
        total = levels * lines
        wide = lines // 4 * span
        chunks = levels // LANES
        dma = pltpu.SemaphoreType.DMA
        heat, advected = pl.pallas_call(
            functools.partial(whole_kernel, nx, ny),
            out_shape=[jax.ShapeDtypeStruct((total, span), f32)] * 2,
            in_specs=[pl.BlockSpec(memory_space=pltpu.VMEM)] * 8,
            out_specs=[pl.BlockSpec(memory_space=pltpu.VMEM)] * 2,
            scratch_shapes=[
                pltpu.VMEM((2, chunks, FIELDS * LANES, wide), f32),
                pltpu.VMEM((2, chunks, FIELDS * LANES, wide), f32),
                pltpu.VMEM((lines, span), f32),
                pltpu.VMEM((lines, span), f32),
                pltpu.VMEM((2, 128, wide), jnp.bfloat16),
                pltpu.VMEM((LANES, 128, wide), jnp.bfloat16),
                pltpu.VMEM((chunks, 3 * gtot, 128), jnp.bfloat16),
                pltpu.VMEM((gtot, 1), f32),
                pltpu.VMEM((3 * gtot, 128), f32),
                pltpu.VMEM((8, 128), f32),
                pltpu.VMEM((128, 128), f32),
                pltpu.VMEM((2, 3 * gtot, wide), f32),
                pltpu.VMEM((gtot, wide), f32),
                pltpu.VMEM((gtot, wide), f32),
                pltpu.VMEM((levels + 1, gtot, wide), f32),
                pltpu.VMEM((levels, gtot, wide), f32),
                pltpu.VMEM((levels, gtot, wide), f32),
                pltpu.VMEM((levels + 8, wide), f32),
                pltpu.VMEM((2, levels, wide), f32),
                pltpu.VMEM((2, levels, wide), f32),
                pltpu.VMEM((total, span), f32),
                pltpu.VMEM((total, span), f32),
                pltpu.VMEM((3, PARTS, 2, levels // PARTS, span), f32),
                pltpu.VMEM((3, PARTS, 2, levels // PARTS, span), f32),
                pltpu.VMEM((3, PARTS, 2, lines, span), f32),
                pltpu.VMEM((3, PARTS, 6, lines, span), f32),
                dma((2, chunks)), dma((2, chunks)), dma(()), dma(()), dma((2,)), dma((2,)),
                dma((3, PARTS, 8)), dma((3, PARTS, 8)),
            ],
            compiler_params=pltpu.CompilerParams(
                vmem_limit_bytes=58 * 2**20, collective_id=0, has_side_effects=True
            ),
            name="shortwave_advection",
        )(
            atmospheric_constituents.reshape(FIELDS * total, span),
            thermal_ratio.reshape(total, span),
            flow_velocity.reshape(2 * total, span),
            solar_elevation_factor,
            ground_reflectivity,
            sunlit_indicator,
            molecular_optics_lookup.transpose(0, 2, 1),
            condensate_optics_lookup,
        )
        heat, advected = pl.pallas_call(
            finish_kernel,
            out_shape=[jax.ShapeDtypeStruct((total, span), f32)] * 2,
            in_specs=[pl.BlockSpec(memory_space=pl.ANY)] * 2,
            out_specs=[pl.BlockSpec(memory_space=pl.ANY)] * 2,
            scratch_shapes=[pltpu.VMEM((2, 2, total // 2, span), f32), dma((2, 2, 2))],
            name="results",
        )(heat, advected)
        return (heat.reshape(levels, lines, span), advected.reshape(levels, lines, span))

    in_specs = (
        P(None, None, "gy", "gx"),
        P(None, "gy", "gx"),
        P(None, None, "gy", "gx"),
        P("gy", "gx"),
        P("gy", "gx"),
        P("gy", "gx"),
        P(),
        P(),
    )
    out_specs = (P(None, "gy", "gx"), P(None, "gy", "gx"))
    return jax.shard_map(local, mesh=mesh, in_specs=in_specs, out_specs=out_specs, check_vma=False)
```

```python
import functools

import jax
import jax.numpy as jnp
import numpy as np
from jax import lax
from jax.experimental import pallas as pl
from jax.experimental.pallas import tpu as pltpu
from jax.sharding import PartitionSpec as P

NODES = 4
TIME_INCREMENT = 0.05
LOG2E = 1.4426950408889634
MESH = pl.DeviceIdType.MESH
FIELDS = 5
LANES = 8
PARTS = 3


def gll_derivative():
    points = np.array([-1.0, -1.0 / np.sqrt(5.0), 1.0 / np.sqrt(5.0), 1.0])
    legendre = 0.5 * (5.0 * points**3 - 3.0 * points)
    derivative = np.zeros((4, 4))
    for source in range(4):
        for target in range(4):
            if source != target:
                derivative[source, target] = legendre[source] / (
                    legendre[target] * (points[source] - points[target])
                )
    derivative[0, 0] = -3.0
    derivative[3, 3] = 3.0
    return derivative


def build_coefs(mol_ref, tab_ref, lhs_ref, w_ref, mols, waters, flip):
    f32 = jnp.float32
    gtot, span = w_ref.shape[0], mols.shape[1]
    levels = mol_ref.shape[1]
    for k in range(3):
        flip[...] = jnp.zeros_like(flip)
        flip[0:levels, 0:gtot] = mol_ref[k]
        mols[k * gtot : (k + 1) * gtot, :] = flip[...].T[0:gtot, :]
    waters[...] = jnp.zeros_like(waters)
    waters[0 : tab_ref.shape[0], 0:gtot] = tab_ref[...]
    table = waters[...].T
    w_ref[...] = table[0:gtot, 6:7]
    tile = 16
    lane = lax.broadcasted_iota(jnp.int32, (tile, span), 1)
    field = lane // LANES

    for i in range(gtot // tile):
        rows = slice(i * tile, (i + 1) * tile)
        lext, lalb, lasy, iext, ialb, iasy = (
            jnp.broadcast_to(table[rows, k : k + 1], (tile, span)) for k in range(6)
        )

        def water(liquid, ice):
            return jnp.where(field == 3, liquid, jnp.where(field == 4, ice, 0.0))

        fixed = [
            water(lext, iext),
            water(lext * (1 - lalb), iext * (1 - ialb)),
            water(lext * lalb * (1 - lasy), iext * ialb * (1 - iasy)),
        ]

        @pl.loop(0, lhs_ref.shape[0])
        def _(c, i=i, fixed=fixed):
            k0, k1, k2 = (
                pltpu.roll(
                    mols[pl.ds(k * gtot + i * tile, tile), :],
                    lax.rem(span + LANES * k - LANES * c, span),
                    1,
                )
                for k in range(3)
            )
            gas = jnp.where(field == 0, k0, jnp.where(field == 1, k1, 0.0))
            rayleigh = jnp.where(field == 2, k2, 0.0)
            sums = [2.0 * (fixed[0] + gas + rayleigh), fixed[1] + gas, fixed[2] + rayleigh]
            for n, value in enumerate(sums):
                high = value.astype(jnp.bfloat16).astype(f32)
                low = value - high
                wide = (
                    high
                    + pltpu.roll(high, FIELDS * LANES, 1)
                    + pltpu.roll(low, 2 * FIELDS * LANES, 1)
                )
                lhs_ref[c, pl.ds(n * gtot + i * tile, tile), :] = wide.astype(jnp.bfloat16)


def shortwave(
    prepare, base_ref, mask_ref, mu, ground, lhs_ref, w_ref, out_ref,
    mm, beam, src, a_all, p_all, o_all, flux,
):
    levels, gtot, n = p_all.shape
    blocks = gtot // 8
    chunks = levels // LANES
    f32 = jnp.float32
    nc = jnp.broadcast_to((-0.5 * LOG2E) / mu, (8, n))

    pieces = 3

    def right_side(l):
        return base_ref[lax.rem(l // LANES, 2)] * mask_ref[lax.rem(l, LANES)]

    def multiply(l, slot, rhs, piece):
        rows = pl.ds(gtot * piece, gtot)
        mm[slot, rows, :] = jnp.dot(
            lhs_ref[l // LANES, rows, :], rhs, preferred_element_type=f32
        )

    prepare(0)
    for piece in range(pieces):
        multiply(0, 0, right_side(0), piece)
    acc = jnp.zeros((8, n), f32)
    for i in range(blocks):
        sl = pl.ds(8 * i, 8)
        first = w_ref[sl, :] * mu
        beam[sl, :] = first
        src[sl, :] = jnp.zeros((8, n), f32)
        a_all[0, sl, :] = jnp.zeros((8, n), f32)
        acc = acc + first
    flux[0:1, :] = jnp.sum(acc, axis=0, keepdims=True)

    def down(l, slot):
        later = jnp.minimum(l + 1, levels - 1)
        rhs = right_side(later)
        acc = jnp.zeros((8, n), f32)
        for i in range(blocks):
            if i % 5 == 0:
                multiply(later, 1 - slot, rhs, i // 5)
            sl = pl.ds(8 * i, 8)
            t2 = mm[slot, sl, :]
            a = mm[slot, pl.ds(gtot + 8 * i, 8), :]
            b = mm[slot, pl.ds(2 * gtot + 8 * i, 8), :]
            bm = beam[sl, :]
            s = src[sl, :]
            alb = a_all[l, sl, :]
            c = a + b
            pr = a * c
            q = pr * lax.rsqrt(pr)
            t = jnp.tanh(q)
            x = a + c
            outer = q * (1.0 / t)
            inner = q * t
            rden = 1.0 / (x + outer + inner)
            refl = b * rden
            tran = (outer - inner) * rden
            bn = bm * jnp.exp2(t2 * nc)
            lost = bm - bn
            w = lost * (1.0 / t2)
            rb = w * b
            tb = lost - w * x
            inv = 1.0 / (1.0 - refl * alb)
            p = tran * inv
            o = (refl * s + rb) * inv
            a1 = refl + (tran * alb) * p
            s1 = tb + p * (s + alb * rb)
            p_all[l, sl, :] = p
            o_all[l, sl, :] = o
            a_all[l + 1, sl, :] = a1
            beam[sl, :] = bn
            src[sl, :] = s1
            acc = acc + (bn + s1)
        flux[pl.ds(l + 1, 1), :] = jnp.sum(acc, axis=0, keepdims=True)

    @pl.loop(0, chunks)
    def _(c):
        @pl.when(c + 1 < chunks)
        def _():
            prepare(c + 1)

        @pl.loop(0, LANES // 2)
        def _(h):
            l = c * LANES + 2 * h
            down(l, 0)
            down(l + 1, 1)

    ups = []
    acc = jnp.zeros((8, n), f32)
    for i in range(blocks):
        sl = pl.ds(8 * i, 8)
        alb = a_all[levels, sl, :]
        up = ground * (src[sl, :] + beam[sl, :]) * (1.0 / (1.0 - ground * alb))
        ups.append(up)
        acc = acc + (1.0 - alb) * up
    last = pl.ds(levels, 1)
    flux[last, :] = flux[last, :] - jnp.sum(acc, axis=0, keepdims=True)

    def upward(k, ups):
        l = levels - 1 - k
        acc = jnp.zeros((8, n), f32)
        out = []
        for i in range(blocks):
            sl = pl.ds(8 * i, 8)
            up = p_all[l, sl, :] * ups[i] + o_all[l, sl, :]
            acc = acc + (1.0 - a_all[l, sl, :]) * up
            out.append(up)
        row = pl.ds(l, 1)
        flux[row, :] = flux[row, :] - jnp.sum(acc, axis=0, keepdims=True)
        return tuple(out)

    lax.fori_loop(0, levels, upward, tuple(ups))
    out_ref[...] = (levels / gtot) * (flux[0:levels, :] - flux[1 : levels + 1, :])


def whole_kernel(
    nx, ny, state_hbm, temp_hbm, flow_hbm, mu_ref, ground_ref, day_ref, mol_ref, tab_ref,
    heat_ref, adv_ref,
    state_ref, temp_ref, flow_ref, loads, snd, got, sfcsnd, sfcgot, base, mask, lhs_ref, w_ref, mols, waters, flip, mm, beam, src, a_all, p_all, o_all, flux, hwork, hgot,
    raw, cur, rowsnd, rowgot, edgesnd, edgegot,
    state_send, state_recv, sfc_send, sfc_recv, heat_send, heat_recv, halo_send, halo_recv,
):
    f32 = jnp.float32
    gx, gy = lax.axis_index("gx"), lax.axis_index("gy")
    lines, span = mu_ref.shape
    total = temp_ref.shape[0]
    levels = total // lines
    half = lines // 2
    pair = half // 2
    east, west = lax.rem(gx + 1, nx), lax.rem(gx + nx - 1, nx)
    south, north = lax.rem(gy + 1, ny), lax.rem(gy + ny - 1, ny)
    far = lax.rem(gx + nx // 2, nx)
    mine = jnp.where(gx < nx // 2, 0, half)
    theirs = half - mine

    targets = [
        (east, gy), (east, south), (east, north),
        (west, gy), (west, south), (west, north),
        (gx, south), (gx, north),
    ]
    inputs = [
        pltpu.make_async_copy(source, sink, loads.at[n])
        for n, (source, sink) in enumerate(
            ((temp_hbm, temp_ref), (state_hbm, state_ref), (flow_hbm, flow_ref))
        )
    ]
    for copy in inputs:
        copy.start()
    barrier = pltpu.get_barrier_semaphore()
    for device in targets + [(far, gy)]:
        pl.semaphore_signal(barrier, inc=1, device_id=device, device_id_type=MESH)
    pl.semaphore_wait(barrier, len(targets) + 1)

    chunks = levels // LANES

    def products(line, c):
        def line_of(ref, k):
            return ref[pl.ds(k * total + c * (LANES * lines) + line, LANES, stride=lines), :]

        temper = line_of(temp_ref, 0)
        thick = line_of(state_ref, 2)
        weighted = thick * temper * temper
        return [
            weighted * line_of(state_ref, 0),
            weighted * line_of(state_ref, 1),
            thick,
            line_of(state_ref, 3),
            line_of(state_ref, 4),
        ]

    def state_copy(h, c):
        return pltpu.make_async_remote_copy(
            src_ref=snd.at[h, c], dst_ref=got.at[h, c], send_sem=state_send.at[h, c],
            recv_sem=state_recv.at[h, c], device_id=(far, gy), device_id_type=MESH,
        )

    surface_copy = pltpu.make_async_remote_copy(
        src_ref=sfcsnd, dst_ref=sfcgot, send_sem=sfc_send, recv_sem=sfc_recv,
        device_id=(far, gy), device_id_type=MESH,
    )

    def heat_copy(h):
        return pltpu.make_async_remote_copy(
            src_ref=hwork.at[h], dst_ref=hgot.at[h], send_sem=heat_send.at[h],
            recv_sem=heat_recv.at[h], device_id=(far, gy), device_id_type=MESH,
        )

    inputs[0].wait()
    inputs[1].wait()
    for n in range(half):
        line = pl.ds(theirs + n, 1)
        sfcsnd[n : n + 1, :] = mu_ref[line, :]
        sfcsnd[half + n : half + n + 1, :] = ground_ref[line, :]
    surface_copy.start()

    def send_state(h, c):
        for r in range(pair):
            for k, value in enumerate(products(theirs + pair * h + r, c)):
                snd[h, c, k * LANES : (k + 1) * LANES, r * span : (r + 1) * span] = value
        state_copy(h, c).start()

    @pl.loop(0, chunks)
    def _(c):
        send_state(0, c)

    build_coefs(mol_ref, tab_ref, lhs_ref, w_ref, mols, waters, flip)
    row_no = lax.broadcasted_iota(jnp.int32, mask.shape[1:], 0)
    for j in range(LANES):
        mask[j] = jnp.where(lax.rem(row_no, LANES) == j, 1.0, 0.0).astype(jnp.bfloat16)

    dref = gll_derivative()
    lane = lax.broadcasted_iota(jnp.int32, (lines, span), 1)
    line_no = lax.broadcasted_iota(jnp.int32, (lines, span), 0)
    node_x, node_y = lane % NODES, line_no % NODES

    def taps(node):
        out = []
        for k in range(1 - NODES, NODES):
            coef = jnp.zeros((lines, span), f32)
            for i in range(NODES):
                if 0 <= i + k < NODES and dref[i, i + k] != 0.0:
                    coef = jnp.where(node == i, float(dref[i, i + k]), coef)
            out.append((k, coef))
        return out

    taps_x, taps_y = taps(node_x), taps(node_y)

    def slope(v, axis, size, table):
        out = None
        for k, coef in table:
            moved = v if k == 0 else pltpu.roll(v, (-k) % size, axis)
            out = coef * moved if out is None else out + coef * moved
        return out

    def at(l):
        return pl.ds(pl.multiple_of(l * lines, lines), lines)

    def wind(v, l):
        return flow_ref[at(l), :] * slope(v, 1, span, taps_x) + flow_ref[
            at(levels + l), :
        ] * slope(v, 0, lines, taps_y)

    group = 8
    inputs[2].wait()

    @pl.loop(0, levels // group)
    def _(j):
        for i in range(group):
            l = j * group + i
            raw[at(l), :] = wind(temp_ref[at(l), :], l)

    surface_copy.wait_recv()
    for h in range(2):
        mus, grounds = [], []
        for r in range(pair):
            line = pl.ds(mine + pair * h + r, 1)
            own = day_ref[line, :] == 1
            n = pair * h + r
            mus.append(jnp.where(own, mu_ref[line, :], sfcgot[n : n + 1, :]))
            grounds.append(
                jnp.where(own, ground_ref[line, :], sfcgot[half + n : half + n + 1, :])
            )

        def prepare(c, h=h):
            state_copy(h, c).wait_recv()
            if h == 0:
                send_state(1, c)
            highs, lows = [[] for _ in range(FIELDS)], [[] for _ in range(FIELDS)]
            for r in range(pair):
                line = mine + pair * h + r
                own = day_ref[pl.ds(line, 1), :] == 1
                for k, value in enumerate(products(line, c)):
                    other = got[h, c, k * LANES : (k + 1) * LANES, r * span : (r + 1) * span]
                    value = jnp.where(own, value, other)
                    high = value.astype(jnp.bfloat16).astype(f32)
                    highs[k].append(high)
                    lows[k].append(value - high)
            highs = [jnp.concatenate(v, axis=1) for v in highs]
            lows = [jnp.concatenate(v, axis=1) for v in lows]
            parts = highs + lows + highs + [jnp.zeros_like(highs[0])]
            base[lax.rem(c, 2)] = jnp.concatenate(parts, axis=0).astype(jnp.bfloat16)

        shortwave(
            prepare, base, mask, jnp.concatenate(mus, axis=1), jnp.concatenate(grounds, axis=1),
            lhs_ref, w_ref, hwork.at[h], mm, beam, src, a_all, p_all, o_all, flux,
        )
        heat_copy(h).start()

    def place(source, first, h):
        for r in range(pair):
            line = first + pair * h + r
            own = day_ref[pl.ds(line, 1), :] == 1
            heat_ref[pl.ds(line, levels, stride=lines), :] = jnp.where(
                own, source[h, :, r * span : (r + 1) * span], 0.0
            )

    for h in range(2):
        place(hwork, mine, h)
    for h in range(2):
        heat_copy(h).wait_recv()
        place(hgot, theirs, h)

    def average(v, before, beyond, node):
        return jnp.where(
            node == NODES - 1, 0.5 * (v + beyond), jnp.where(node == 0, 0.5 * (before + v), v)
        )

    def average_y(v, above, under):
        before = jnp.where(line_no == 0, above, pltpu.roll(v, 1, 0))
        beyond = jnp.where(line_no == lines - 1, under, pltpu.roll(v, lines - 1, 0))
        return average(v, before, beyond, node_y)

    parts = rowsnd.shape[1]
    depth = levels // parts
    steps = depth // group

    def halo_copies(stage, g):
        copies = []
        for n, device in enumerate(targets):
            if n < 6:
                source, sink = edgesnd.at[stage, g, 1 - n // 3], edgegot.at[stage, g, n]
            else:
                source, sink = rowsnd.at[stage, g, 7 - n], rowgot.at[stage, g, n - 6]
            copies.append(
                pltpu.make_async_remote_copy(
                    src_ref=source, dst_ref=sink, send_sem=halo_send.at[stage, g, n],
                    recv_sem=halo_recv.at[stage, g, n], device_id=device, device_id_type=MESH,
                )
            )
        return copies

    def emit(stage, g):
        def prepare(j, edges):
            west_edge, east_edge = edges
            for i in range(group):
                l = g * depth + j * group + i
                if stage == 0:
                    value = heat_ref[at(l), :] - raw[at(l), :]
                else:
                    value = heat_ref[at(l), :] - wind(cur[at(l), :], l)
                raw[at(l), :] = value
                here = lane == l
                west_edge = jnp.where(here, pltpu.roll(value, l, 1), west_edge)
                east_edge = jnp.where(here, pltpu.roll(value, l + 1, 1), east_edge)
            return west_edge, east_edge

        nothing = jnp.zeros((lines, span), f32)
        west_edge, east_edge = lax.fori_loop(0, steps, prepare, (nothing, nothing))
        edgesnd[stage, g, 0] = west_edge
        edgesnd[stage, g, 1] = east_edge
        for side, line in enumerate((0, lines - 1)):
            rowsnd[stage, g, side] = raw[pl.ds(g * depth * lines + line, depth, stride=lines), :]
        for copy in halo_copies(stage, g):
            copy.start()

    def absorb(stage, g):
        for copy in halo_copies(stage, g):
            copy.wait_recv()
        beside = [
            average_y(
                edgegot[stage, g, 3 * side],
                edgegot[stage, g, 3 * side + 1, lines - 1 : lines, :],
                edgegot[stage, g, 3 * side + 2, 0:1, :],
            )
            for side in range(2)
        ]

        def finish(j, carry):
            for i in range(group):
                k = j * group + i
                l = g * depth + k
                value = average_y(
                    raw[at(l), :],
                    rowgot[stage, g, 0, pl.ds(k, 1), :],
                    rowgot[stage, g, 1, pl.ds(k, 1), :],
                )
                before = jnp.where(
                    lane == 0, pltpu.roll(beside[0], span - l, 1), pltpu.roll(value, 1, 1)
                )
                beyond = jnp.where(
                    lane == span - 1,
                    pltpu.roll(beside[1], span - 1 - l, 1),
                    pltpu.roll(value, span - 1, 1),
                )
                step = TIME_INCREMENT * average(value, before, beyond, node_x)
                start = temp_ref[at(l), :]
                if stage == 0:
                    cur[at(l), :] = start + step
                elif stage == 1:
                    cur[at(l), :] = 0.75 * start + 0.25 * (cur[at(l), :] + step)
                else:
                    adv_ref[at(l), :] = 1.0 / 3.0 * start + 2.0 / 3.0 * (cur[at(l), :] + step)
            return carry

        lax.fori_loop(0, steps, finish, 0)

    for g in range(parts):
        emit(0, g)
    for stage in range(3):
        for g in range(parts):
            absorb(stage, g)
            if stage < 2:
                emit(stage + 1, g)
    for stage in range(3):
        for g in range(parts):
            for copy in halo_copies(stage, g):
                copy.wait_send()
    surface_copy.wait_send()
    for h in range(2):
        heat_copy(h).wait_send()

        @pl.loop(0, chunks)
        def _(c, h=h):
            state_copy(h, c).wait_send()


def finish_kernel(heat_ref, adv_ref, heat_out, adv_out, hold, sems):
    rows = hold.shape[2]
    stages = []
    for n, (source, sink) in enumerate(((heat_ref, heat_out), (adv_ref, adv_out))):
        for part in range(hold.shape[1]):
            here = pl.ds(part * rows, rows)
            keep = hold.at[n, part]
            stages.append(
                (
                    pltpu.make_async_copy(source.at[here], keep, sems.at[0, n, part]),
                    pltpu.make_async_copy(keep, sink.at[here], sems.at[1, n, part]),
                )
            )
    for first, _ in stages:
        first.start()
    for first, second in stages:
        first.wait()
        second.start()
    for _, second in stages:
        second.wait()


def solution(mesh):
    nx, ny = mesh.shape["gx"], mesh.shape["gy"]

    def local(
        atmospheric_constituents,
        thermal_ratio,
        flow_velocity,
        solar_elevation_factor,
        ground_reflectivity,
        sunlit_indicator,
        molecular_optics_lookup,
        condensate_optics_lookup,
    ):
        f32 = jnp.float32
        levels, lines, span = thermal_ratio.shape
        gtot = condensate_optics_lookup.shape[1]
        total = levels * lines
        wide = lines // 4 * span
        chunks = levels // LANES
        dma = pltpu.SemaphoreType.DMA
        heat, advected = pl.pallas_call(
            functools.partial(whole_kernel, nx, ny),
            out_shape=[jax.ShapeDtypeStruct((total, span), f32)] * 2,
            in_specs=[pl.BlockSpec(memory_space=pl.ANY)] * 3
            + [pl.BlockSpec(memory_space=pltpu.VMEM)] * 5,
            out_specs=[pl.BlockSpec(memory_space=pltpu.VMEM)] * 2,
            scratch_shapes=[
                pltpu.VMEM((FIELDS * total, span), f32),
                pltpu.VMEM((total, span), f32),
                pltpu.VMEM((2 * total, span), f32),
                dma((3,)),
                pltpu.VMEM((2, chunks, FIELDS * LANES, wide), f32),
                pltpu.VMEM((2, chunks, FIELDS * LANES, wide), f32),
                pltpu.VMEM((lines, span), f32),
                pltpu.VMEM((lines, span), f32),
                pltpu.VMEM((2, 128, wide), jnp.bfloat16),
                pltpu.VMEM((LANES, 128, wide), jnp.bfloat16),
                pltpu.VMEM((chunks, 3 * gtot, 128), jnp.bfloat16),
                pltpu.VMEM((gtot, 1), f32),
                pltpu.VMEM((3 * gtot, 128), f32),
                pltpu.VMEM((8, 128), f32),
                pltpu.VMEM((128, 128), f32),
                pltpu.VMEM((2, 3 * gtot, wide), f32),
                pltpu.VMEM((gtot, wide), f32),
                pltpu.VMEM((gtot, wide), f32),
                pltpu.VMEM((levels + 1, gtot, wide), f32),
                pltpu.VMEM((levels, gtot, wide), f32),
                pltpu.VMEM((levels, gtot, wide), f32),
                pltpu.VMEM((levels + 8, wide), f32),
                pltpu.VMEM((2, levels, wide), f32),
                pltpu.VMEM((2, levels, wide), f32),
                pltpu.VMEM((total, span), f32),
                pltpu.VMEM((total, span), f32),
                pltpu.VMEM((3, PARTS, 2, levels // PARTS, span), f32),
                pltpu.VMEM((3, PARTS, 2, levels // PARTS, span), f32),
                pltpu.VMEM((3, PARTS, 2, lines, span), f32),
                pltpu.VMEM((3, PARTS, 6, lines, span), f32),
                dma((2, chunks)), dma((2, chunks)), dma(()), dma(()), dma((2,)), dma((2,)),
                dma((3, PARTS, 8)), dma((3, PARTS, 8)),
            ],
            compiler_params=pltpu.CompilerParams(
                vmem_limit_bytes=58 * 2**20, collective_id=0, has_side_effects=True
            ),
            name="shortwave_advection",
        )(
            atmospheric_constituents.reshape(FIELDS * total, span),
            thermal_ratio.reshape(total, span),
            flow_velocity.reshape(2 * total, span),
            solar_elevation_factor,
            ground_reflectivity,
            sunlit_indicator,
            molecular_optics_lookup.transpose(0, 2, 1),
            condensate_optics_lookup,
        )
        heat, advected = pl.pallas_call(
            finish_kernel,
            out_shape=[jax.ShapeDtypeStruct((total, span), f32)] * 2,
            in_specs=[pl.BlockSpec(memory_space=pl.ANY)] * 2,
            out_specs=[pl.BlockSpec(memory_space=pl.ANY)] * 2,
            scratch_shapes=[pltpu.VMEM((2, 2, total // 2, span), f32), dma((2, 2, 2))],
            name="results",
        )(heat, advected)
        return (heat.reshape(levels, lines, span), advected.reshape(levels, lines, span))

    in_specs = (
        P(None, None, "gy", "gx"),
        P(None, "gy", "gx"),
        P(None, None, "gy", "gx"),
        P("gy", "gx"),
        P("gy", "gx"),
        P("gy", "gx"),
        P(),
        P(),
    )
    out_specs = (P(None, "gy", "gx"), P(None, "gy", "gx"))
    return jax.shard_map(local, mesh=mesh, in_specs=in_specs, out_specs=out_specs, check_vma=False)
```
